512 devices in a mesh: seq: 64 (over z, y), tp: 8 (over x, core).
Axes of the slice: x: 4, y: 4, z: 16, core: 2. Of those that a mesh axis runs over, the one named last changes fastest.
Arguments:
- query_proj: bfloat16 [4096, 8192], P('tp', 'seq'), may hold values from -6 to 6
- key_proj: bfloat16 [4096, 8192], P('tp', 'seq'), may hold values from -6 to 6
- value_proj: bfloat16 [4096, 8192], P('tp', 'seq'), may hold values from -6 to 6
- short_taps: float32 [3, 3, 4096], P(None, None, 'tp'), may hold values from -3.5 to 3.5
- long_filters: float32 [4096, 8192], P(('tp', 'seq')), may hold values from -2 to 2
- out_weight: bfloat16 [4096, 8192], P('seq', 'tp'), may hold values from -0.09375 to 0.09375
Outputs:
- block_out: bfloat16 [8192, 8192], P('seq', 'tp')
The draws below stay inside these ranges and needn't reach their ends.
All inputs are finite; a program needn't handle non-finite values.
Results may differ from the reference program's by a relative error of at most 0.0058.
Values may be sent and summed in bfloat16 or wider, within the bound.
A program may use at most 64 MiB of HBM per device.

```python
import jax
import jax.numpy as jnp
from jax import lax

D = 8192
CONV_CHANNELS = 4096
SEQUENCE_LENGTH = 8192


def draw_long_filters(key, part):
    random_splits = jax.random.split(key, 6)
    noisy_component = jax.random.truncated_normal(random_splits[0], -4.0, 4.0, (CONV_CHANNELS, SEQUENCE_LENGTH), jnp.float32)
    slow_share = 0.5
    is_slow = jax.random.uniform(random_splits[1], (CONV_CHANNELS, 1), jnp.float32) < slow_share
    slow_rate = jnp.log(10.0) / SEQUENCE_LENGTH * jnp.exp(jax.random.uniform(random_splits[2], (CONV_CHANNELS, 1), jnp.float32, jnp.log(0.05), jnp.log(0.5)))
    fast_rate = jnp.log(10.0) / jax.random.uniform(random_splits[3], (CONV_CHANNELS, 1), jnp.float32, 30.0, 50.0)
    falloff_speed = jnp.where(is_slow, slow_rate, fast_rate)
    filter_offset = jnp.arange(SEQUENCE_LENGTH, dtype=jnp.float32)[None, :]
    spike_location = jax.random.uniform(random_splits[4], (CONV_CHANNELS, 2), jnp.float32) * SEQUENCE_LENGTH
    spike_retained = jax.random.uniform(random_splits[5], (CONV_CHANNELS, 2), jnp.float32, 0.5, 0.8)
    filter_spikes = jnp.where(filter_offset >= spike_location[:, 0:1], spike_retained[:, 0:1], 1.0) * jnp.where(filter_offset >= spike_location[:, 1:2], spike_retained[:, 1:2], 1.0)
    norm_divisor = jnp.sqrt(2.0 * falloff_speed / (1.0 - jnp.exp(-2.0 * falloff_speed * SEQUENCE_LENGTH)))
    return (noisy_component * jnp.exp(-falloff_speed * filter_offset) * filter_spikes * norm_divisor).astype(jnp.float32)


def level_of(rng, dims, cuts, smallest, largest):
    level, own = 1.0, jax.random.fold_in(rng, 6)
    for dim, shards_of in cuts:
        draws = jnp.exp(jax.random.uniform(jax.random.fold_in(own, dim), (shards_of,), jnp.float32, smallest / len(cuts), largest / len(cuts)))
        level = level * jnp.repeat(draws, dims[dim] // shards_of).reshape([-1 if axis == dim else 1 for axis in range(len(dims))])
    return level


def normal_values(key, shape, deviation, limit, cuts=(), held_as=jnp.bfloat16):
    array = deviation * jax.random.normal(key, shape, jnp.float32)
    if cuts:
        array = array * level_of(key, shape, cuts, -0.22, 0.18)
    return jnp.clip(array, -limit, limit).astype(held_as)


def setup_inputs(seed: int = 0) -> dict:
    keys = jax.random.split(jax.random.key(seed), 7)
    query_proj = normal_values(keys[0], (CONV_CHANNELS, SEQUENCE_LENGTH), 1.0, 6.0, ((0, 8), (1, 64)))
    key_proj = normal_values(keys[1], (CONV_CHANNELS, SEQUENCE_LENGTH), 1.0, 6.0, ((0, 8), (1, 64)))
    value_proj = normal_values(keys[2], (CONV_CHANNELS, SEQUENCE_LENGTH), 1.0, 6.0, ((0, 8), (1, 64)))
    short_taps = normal_values(keys[3], (3, 3, CONV_CHANNELS), 3 ** -0.5, 3.5, ((2, 8),), jnp.float32)
    long_filters = draw_long_filters(jax.random.fold_in(keys[6], 71), 0)
    out_weight = normal_values(keys[5], (CONV_CHANNELS, D), CONV_CHANNELS ** -0.5, 0.09375, ((0, 64), (1, 8)))
    return {"query_proj": query_proj, "key_proj": key_proj, "value_proj": value_proj, "short_taps": short_taps, "long_filters": long_filters, "out_weight": out_weight}


def short_filter(extended, tap_weights):
    return (tap_weights[0][:, None] * extended[:, 2:]
            + tap_weights[1][:, None] * extended[:, 1:-1]
            + tap_weights[2][:, None] * extended[:, :-2])


def convolve_block(block_pair):
    product_block, filter_block = block_pair
    padded_len = 2 * SEQUENCE_LENGTH
    spectrum = jnp.fft.rfft(product_block, n=padded_len, axis=1) * jnp.fft.rfft(filter_block, n=padded_len, axis=1)
    return jnp.fft.irfft(spectrum, n=padded_len, axis=1)[:, :SEQUENCE_LENGTH].astype(product_block.dtype)


def reference(query_proj, key_proj, value_proj, short_taps, long_filters, out_weight):
    shorts = []
    for stream_index, stream in enumerate((query_proj, key_proj, value_proj)):
        extended = jnp.pad(stream.astype(jnp.float32), ((0, 0), (2, 0)))
        shorts.append(short_filter(extended, short_taps[stream_index]))
    query_short, key_short, value_short = shorts
    product = lax.optimization_barrier((key_short * value_short).astype(jnp.bfloat16)).astype(jnp.float32)
    block_rows = 32
    mixed_conv = lax.map(convolve_block, (product.reshape(CONV_CHANNELS // block_rows, block_rows, SEQUENCE_LENGTH),
                                          long_filters.reshape(CONV_CHANNELS // block_rows, block_rows, SEQUENCE_LENGTH)))
    mixed_conv = mixed_conv.reshape(CONV_CHANNELS, SEQUENCE_LENGTH)
    gated_out = (query_short * mixed_conv).astype(jnp.bfloat16)
    result = lax.dot_general(gated_out, out_weight, (((0,), (0,)), ((), ())), preferred_element_type=jnp.float32)
    return result.astype(jnp.bfloat16)
```

```python
import functools
import math

import jax
import jax.numpy as jnp
import numpy as np
from jax import lax
from jax.experimental import pallas as pl
from jax.experimental.pallas import tpu as pltpu
from jax.sharding import PartitionSpec as P

MESH = pl.DeviceIdType.MESH
F32 = jnp.float32
BF16 = jnp.bfloat16
BLOCK = 128
OWN = 8
exact = functools.partial(jnp.dot, precision=lax.Precision.HIGHEST, preferred_element_type=F32)


def tables(blocks):
    period = 2 * blocks * BLOCK
    padded = -(-(blocks + 1) // 8) * 8
    kb = np.arange(padded)[:, None]
    live = kb <= blocks
    left = 2 * math.pi * (kb * np.arange(blocks)[None, :] % (2 * blocks)) / (2 * blocks)
    forward = np.concatenate([live * np.cos(left), -(live * np.sin(left))], axis=0)
    share = np.where((kb == 0) | (kb == blocks), 1.0, 2.0) * live / period
    inverse = np.concatenate([share * np.cos(left), -(share * np.sin(left))], axis=0).T
    twist = 2 * math.pi * (kb * np.arange(BLOCK)[None, :] % period) / period
    turn = np.stack([np.cos(twist), -np.sin(twist)])
    right = np.arange(BLOCK)
    right = 2 * math.pi * (right[:, None] * right[None, :] % BLOCK) / BLOCK
    c, s = np.cos(right), np.sin(right)
    rows = np.block([[c, -s], [s, c]])
    return [np.asarray(a, np.float32) for a in (forward, inverse, turn, rows, np.ascontiguousarray(rows.T))]


def kernel(
    nz, ny, nx,
    q_ref, k_ref, v_ref, taps_ref, h_ref, w_ref,
    fwd_ref, inv_ref, turn_ref, rf_ref, ri_ref,
    out_ref,
    wide, edge_s, edge_r, prod, qout, yr, qr, zs, xin, rows, spec, ms, ar, gt, ga, wg, ps, pr, total,
    edge_sem, y_sem, z_send, z_recv, c_send, c_recv, x_send, x_recv, b_send, b_recv,
    w_send, w_recv, r_send, r_recv, own_sem,
):
    nc = 2
    nb = nz * ny
    ntp = nx * nc
    group = OWN * ntp
    seq = lax.axis_index("seq")
    tp = lax.axis_index("tp")
    z, y = seq // ny, seq % ny
    x, core = tp // nc, tp % nc

    def at(zz, yy):
        return (zz * ny + yy, tp)

    barrier = pltpu.get_barrier_semaphore()

    @pl.loop(1, nb)
    def _(d):
        pl.semaphore_signal(barrier, inc=1, device_id=((seq + d) % nb, tp), device_id_type=MESH)

    for d in range(1, nx):
        pl.semaphore_signal(barrier, inc=1, device_id=(seq, (x + d) % nx * nc + core), device_id_type=MESH)
    sibling = (seq, x * nc + (1 - core))
    pl.semaphore_signal(barrier, inc=1, device_id=sibling, device_id_type=MESH)

    def remote(src, dst, send, recv, target):
        return pltpu.make_async_remote_copy(
            src_ref=src, dst_ref=dst, send_sem=send, recv_sem=recv, device_id=target, device_id_type=MESH
        )

    own_w = pltpu.make_async_copy(w_ref, wg.at[z], own_sem.at[0])
    own_w.start()
    half = group // 2

    def ring_copy(way, r, h):
        step = 1 if way == 0 else -1
        origin = (z - step * (r - 1) + nz) % nz
        cut = pl.ds(h * half, half)
        src = w_ref.at[cut] if r == 1 else wg.at[origin, cut]
        return remote(src, wg.at[origin, cut], w_send.at[way, r - 1, h], w_recv.at[way, r - 1, h],
                      at((z + step + nz) % nz, y))

    last = (nz // 2, nz - 1 - nz // 2)

    def ring(r):
        for h in range(2):
            for way in range(2):
                if 2 <= r <= last[way] + 1:
                    ring_copy(way, r - 1, h).wait_recv()
                if r <= last[way]:
                    ring_copy(way, r, h).start()

    wide[...] = jnp.zeros_like(wide)
    for i in range(3):
        wide[3 * i:3 * i + 3, :] = taps_ref[i]
    taps = jnp.transpose(wide[...])

    lane16 = lax.broadcasted_iota(jnp.int32, (16, BLOCK), 1)
    row16 = lax.broadcasted_iota(jnp.int32, (16, BLOCK), 0)
    edge = jnp.zeros((16, OWN * nb), F32)
    for i, ref in enumerate((q_ref, k_ref, v_ref)):
        pick = ((row16 == 2 * i) & (lane16 == BLOCK - 1)) | ((row16 == 2 * i + 1) & (lane16 == BLOCK - 2))
        edge += lax.dot_general(pick.astype(F32).astype(BF16), ref[...], (((1,), (1,)), ((), ())),
                                preferred_element_type=F32)
    edge_s[...] = edge.astype(BF16)

    pad = fwd_ref.shape[0] // 2

    def spectrum():
        columns = jnp.concatenate([rows[pl.ds(c, nb, stride=OWN), :] for c in range(OWN)], axis=1)
        left = exact(fwd_ref[...], columns)
        turned = []
        for c in range(OWN):
            re, im = left[:pad, c * BLOCK:(c + 1) * BLOCK], left[pad:, c * BLOCK:(c + 1) * BLOCK]
            turned.append(jnp.concatenate([re * turn_ref[0] - im * turn_ref[1],
                                           re * turn_ref[1] + im * turn_ref[0]], axis=1))
        return exact(jnp.concatenate(turned, axis=0), rf_ref[...])

    for b in range(nb):
        rows[b * OWN:(b + 1) * OWN, :] = h_ref[:, b * BLOCK:(b + 1) * BLOCK]
    spec[...] = spectrum()

    pl.semaphore_wait(barrier, nb - 1 + nx)

    edge_copy = remote(edge_s, edge_r, edge_sem.at[0], edge_sem.at[1], ((seq + 1) % nb, tp))
    edge_copy.start()
    ring(1)
    edge_copy.wait_recv()

    wide[0:16, :] = edge_r[...].astype(F32) * jnp.where(seq > 0, 1.0, 0.0).astype(F32)
    before = jnp.transpose(wide[...])

    span = min(128, OWN * nb)
    lane = lax.broadcasted_iota(jnp.int32, (span, BLOCK), 1)
    for at_row in range(0, OWN * nb, span):
        cut = slice(at_row, at_row + span)
        shorts = []
        for i, ref in enumerate((q_ref, k_ref, v_ref)):
            now = ref[cut, :].astype(F32)
            one = jnp.where(lane == 0, before[cut, 2 * i:2 * i + 1], pltpu.roll(now, 1, 1))
            two = jnp.where(lane == 0, before[cut, 2 * i + 1:2 * i + 2],
                            jnp.where(lane == 1, before[cut, 2 * i:2 * i + 1], pltpu.roll(now, 2, 1)))
            shorts.append(taps[cut, 3 * i:3 * i + 1] * now + taps[cut, 3 * i + 1:3 * i + 2] * one
                          + taps[cut, 3 * i + 2:3 * i + 3] * two)
        pair = shorts[1] * shorts[2]
        zs_here = span // (OWN * ny)
        for yy in range(ny):
            part = jnp.concatenate([pair[(i * ny + yy) * OWN:(i * ny + yy + 1) * OWN] for i in range(zs_here)], axis=0)
            first = at_row // ny
            prod[yy, first:first + zs_here * OWN, :] = part.astype(BF16)
        for j in range(span // group):
            index = at_row // group + j
            qout[index % ny, (index // ny) * group:(index // ny + 1) * group, :] = (
                shorts[0][j * group:(j + 1) * group].astype(BF16))

    def y_copy(what, d):
        yy = (y + d) % ny
        src, dst = ((prod, yr), (qout, qr))[what]
        return remote(src.at[yy], dst.at[y], y_sem.at[what, 0, d], y_sem.at[what, 1, d], at(z, yy))

    own_y = [pltpu.make_async_copy(src.at[y], dst.at[y], own_sem.at[1 + j])
             for j, (src, dst) in enumerate(((prod, yr), (qout, qr)))]
    for what in range(2):
        own_y[what].start()
        for d in range(1, ny):
            y_copy(what, d).start()
    own_y[0].wait()
    for d in range(1, ny):
        y_copy(0, d).wait_recv()

    for zz in range(nz):
        zs[zz] = jnp.concatenate([yr[yy, pl.ds(zz * OWN // 16 * 16, 16), :].astype(F32)[zz * OWN % 16:zz * OWN % 16 + OWN]
                                  for yy in range(ny)], axis=0).astype(BF16)

    def z_copy(d):
        zz = (z + d) % nz
        return remote(zs.at[zz], xin.at[z], z_send.at[d], z_recv.at[d], at(zz, y))

    own_z = pltpu.make_async_copy(zs.at[z], xin.at[z], own_sem.at[3])
    own_z.start()

    @pl.loop(1, nz)
    def _(d):
        z_copy(d).start()

    for r in range(2, min(4, nz // 2 + 1)):
        ring(r)
    own_z.wait()

    @pl.loop(1, nz)
    def _(d):
        z_copy(d).wait_recv()

    for zz in range(nz):
        rows[zz * ny * OWN:(zz + 1) * ny * OWN, :] = xin[zz].astype(F32)
    data = spectrum()
    dr, di = data[:, :BLOCK], data[:, BLOCK:]
    fr, fi = spec[:, :BLOCK], spec[:, BLOCK:]
    mid = exact(jnp.concatenate([dr * fr - di * fi, dr * fi + di * fr], axis=1), ri_ref[...])
    turned = []
    for c in range(OWN):
        re, im = mid[c * pad:(c + 1) * pad, :BLOCK], mid[c * pad:(c + 1) * pad, BLOCK:]
        turned.append(jnp.concatenate([re * turn_ref[0] + im * turn_ref[1],
                                       im * turn_ref[0] - re * turn_ref[1]], axis=0))
    conv = exact(inv_ref[...], jnp.concatenate(turned, axis=1))
    for c in range(OWN):
        rows[pl.ds(c, nb, stride=OWN), :] = conv[:, c * BLOCK:(c + 1) * BLOCK]
    for zz in range(nz):
        ms[zz] = rows[zz * ny * OWN:(zz + 1) * ny * OWN, :].astype(BF16)

    to_y = z // 2 % ny
    my_slot = ((z // (2 * ny)) * 2 + z % 2) * ny + y

    def c_copy(d):
        zz = (z + d) % nz
        return remote(ms.at[zz], ar.at[my_slot], c_send.at[d], c_recv.at[my_slot], at(zz, to_y))

    @pl.loop(1, nz)
    def _(d):
        c_copy(d).start()

    here = pltpu.make_async_copy(ms.at[z], ar.at[my_slot], c_recv.at[my_slot])

    @pl.when(to_y == y)
    def _():
        here.start()

    @pl.when(to_y != y)
    def _():
        c_copy(0).start()

    for r in range(4, min(6, nz // 2 + 1)):
        ring(r)
    own_y[1].wait()
    for d in range(1, ny):
        y_copy(1, d).wait_recv()

    @pl.loop(0, nz)
    def _(slot):
        pltpu.make_async_copy(ms.at[0], ar.at[slot], c_recv.at[slot]).wait()

    for yy in range(ny):
        part = []
        for slot in range(nz):
            got = ar[slot, yy * OWN // 16 * 16:yy * OWN // 16 * 16 + 16, :].astype(F32)
            part.append(got[yy * OWN % 16:yy * OWN % 16 + OWN])
        mixed = jnp.concatenate(part, axis=0)
        gated = qr[yy].astype(F32) * mixed
        if nz * OWN < BLOCK:
            gated = jnp.concatenate([gated] * (BLOCK // (nz * OWN)), axis=0)
        gt[yy * BLOCK:(yy + 1) * BLOCK, :] = jnp.transpose(gated).astype(BF16)

    def x_copy(d):
        xx = (x + d) % nx
        return remote(gt, ga.at[tp], x_send.at[d], x_recv.at[d], (seq, xx * nc + core))

    def b_copy(d):
        slot = (x - d + nx) % nx * nc + core
        return remote(gt if d == 0 else ga.at[slot], ga.at[slot], b_send.at[d], b_recv.at[d], sibling)

    own_g = pltpu.make_async_copy(gt, ga.at[tp], own_sem.at[4])
    for d in range(1, nx):
        x_copy(d).start()
    b_copy(0).start()
    own_g.start()
    for r in range(6, nz // 2 + 2):
        ring(r)
    if nz // 2 + 2 <= 6:
        for r in range(min(6, nz // 2 + 1), nz // 2 + 2):
            ring(r)
    for d in range(1, nx):
        x_copy(d).wait_recv()
        b_copy(d).start()
    own_g.wait()
    own_w.wait()
    for d in range(nx):
        b_copy(d).wait_recv()

    depth = nz * OWN
    columns = out_ref.shape[1]
    tile = min(256, columns)

    def partial_sum(yy, start):
        lhs = jnp.concatenate([ga[p, pl.ds(pl.multiple_of(yy * BLOCK, BLOCK), BLOCK), :][:, :depth] for p in range(ntp)],
                              axis=1)
        return jnp.dot(lhs, wg[:, :, pl.ds(start, tile)].reshape(nz * group, tile), preferred_element_type=F32)

    def r_copy(d):
        return remote(ps.at[d], pr.at[d], r_send.at[d], r_recv.at[d], at(z, (y + d) % ny))

    for d in list(range(1, ny)):
        @pl.loop(0, columns // tile)
        def _(n):
            start = pl.multiple_of(n * tile, tile)
            ps[d, :, pl.ds(start, tile)] = partial_sum((y + d) % ny, start).astype(BF16)
        r_copy(d).start()

    @pl.loop(0, columns // tile)
    def _(n):
        start = pl.multiple_of(n * tile, tile)
        total[:, pl.ds(start, tile)] = partial_sum(y, start)

    for d in range(1, ny):
        r_copy(d).wait_recv()
    sums = total[...]
    for d in range(1, ny):
        sums += pr[d].astype(F32)
    out_ref[...] = sums.astype(BF16)

    edge_copy.wait_send()
    for way in range(2):
        for r in range(1, last[way] + 1):
            for h in range(2):
                ring_copy(way, r, h).wait_send()
    for what in range(2):
        for d in range(1, ny):
            y_copy(what, d).wait_send()

    @pl.loop(1, nz)
    def _(d):
        z_copy(d).wait_send()
        c_copy(d).wait_send()

    @pl.when(to_y != y)
    def _():
        c_copy(0).wait_send()

    for d in range(1, nx):
        x_copy(d).wait_send()
    for d in range(nx):
        b_copy(d).wait_send()
    for d in range(1, ny):
        r_copy(d).wait_send()


def build(mesh, nz, ny, nx):
    nb, ntp = nz * ny, nx * 2
    held = OWN * nb
    group = OWN * ntp
    consts = tables(nb)

    def shards(query_proj, key_proj, value_proj, short_taps, long_filters, out_weight):
        columns = out_weight.shape[1]
        pad = consts[0].shape[0] // 2
        dma = pltpu.SemaphoreType.DMA
        vmem = pltpu.VMEM
        return pl.pallas_call(
            functools.partial(kernel, nz, ny, nx),
            out_shape=jax.ShapeDtypeStruct((BLOCK, columns), BF16),
            in_specs=[pl.BlockSpec(memory_space=pltpu.VMEM)] * 11,
            out_specs=pl.BlockSpec(memory_space=pltpu.VMEM),
            scratch_shapes=[
                vmem((BLOCK, held), F32),
                vmem((16, held), BF16),
                vmem((16, held), BF16),
                vmem((ny, nz * OWN, BLOCK), BF16),
                vmem((ny, nz * OWN, BLOCK), BF16),
                vmem((ny, nz * OWN, BLOCK), BF16),
                vmem((ny, nz * OWN, BLOCK), BF16),
                vmem((nz, ny * OWN, BLOCK), BF16),
                vmem((nz, ny * OWN, BLOCK), BF16),
                vmem((held, BLOCK), F32),
                vmem((OWN * pad, 2 * BLOCK), F32),
                vmem((nz, ny * OWN, BLOCK), BF16),
                vmem((nz, ny * OWN, BLOCK), BF16),
                vmem((ny * BLOCK, BLOCK), BF16),
                vmem((ntp, ny * BLOCK, BLOCK), BF16),
                vmem((nz, group, columns), BF16),
                vmem((ny, BLOCK, columns), BF16),
                vmem((ny, BLOCK, columns), BF16),
                vmem((BLOCK, columns), F32),
                dma((2,)),
                dma((2, 2, ny)),
                dma((nz,)),
                dma((nz,)),
                dma((nz,)),
                dma((nz,)),
                dma((nx,)),
                dma((nx,)),
                dma((nx,)),
                dma((nx,)),
                dma((2, nz // 2, 2)),
                dma((2, nz // 2, 2)),
                dma((ny,)),
                dma((ny,)),
                dma((5,)),
            ],
            compiler_params=pltpu.CompilerParams(
                collective_id=0, has_side_effects=True, vmem_limit_bytes=60 * 1024 * 1024
            ),
        )(query_proj, key_proj, value_proj, short_taps, long_filters, out_weight, *[jnp.asarray(a) for a in consts])

    return jax.shard_map(
        shards,
        mesh=mesh,
        in_specs=(
            P("tp", "seq"),
            P("tp", "seq"),
            P("tp", "seq"),
            P(None, None, "tp"),
            P(("tp", "seq"), None),
            P("seq", "tp"),
        ),
        out_specs=P("seq", "tp"),
        check_vma=False,
    )


def solution(mesh):
    return build(mesh, mesh.shape["seq"] // 4, 4, mesh.shape["tp"] // 2)
```

```python
import functools
import math

import jax
import jax.numpy as jnp
import numpy as np
from jax import lax
from jax.experimental import pallas as pl
from jax.experimental.pallas import tpu as pltpu
from jax.sharding import PartitionSpec as P

MESH = pl.DeviceIdType.MESH
F32 = jnp.float32
BF16 = jnp.bfloat16
BLOCK = 128
OWN = 8
exact = functools.partial(jnp.dot, precision=lax.Precision.HIGHEST, preferred_element_type=F32)


def tables(blocks):
    period = 2 * blocks * BLOCK
    padded = -(-(blocks + 1) // 8) * 8
    kb = np.arange(padded)[:, None]
    live = kb <= blocks
    left = 2 * math.pi * (kb * np.arange(blocks)[None, :] % (2 * blocks)) / (2 * blocks)
    forward = np.concatenate([live * np.cos(left), -(live * np.sin(left))], axis=0)
    share = np.where((kb == 0) | (kb == blocks), 1.0, 2.0) * live / period
    inverse = np.concatenate([share * np.cos(left), -(share * np.sin(left))], axis=0).T
    twist = 2 * math.pi * (kb * np.arange(BLOCK)[None, :] % period) / period
    turn = np.stack([np.cos(twist), -np.sin(twist)])
    right = np.arange(BLOCK)
    right = 2 * math.pi * (right[:, None] * right[None, :] % BLOCK) / BLOCK
    c, s = np.cos(right), np.sin(right)
    rows = np.block([[c, -s], [s, c]])
    return [np.asarray(a, np.float32) for a in (forward, inverse, turn, rows, np.ascontiguousarray(rows.T))]


def kernel(
    nz, ny, nx,
    q_ref, k_ref, v_ref, taps_ref, h_ref, w_ref,
    fwd_ref, inv_ref, turn_ref, rf_ref, ri_ref,
    out_ref,
    wide, tapst, edge_s, edge_r, raw, got, qs, zs, xin, rows, spec, ms, ar, ga, wp, wg, ps, half_r, pr, total,
    e_sem, y_send, y_recv, wy_send, wy_recv, z_send, z_recv, c_send, c_recv, x_send, x_recv, b_send, b_recv,
    w_send, w_recv, r_send, r_recv, own_sem,
):
    nc = 2
    nb = nz * ny
    ntp = nx * nc
    held = nz * OWN
    seq = lax.axis_index("seq")
    tp = lax.axis_index("tp")
    z, y = seq // ny, seq % ny
    x, core = tp // nc, tp % nc

    def at(zz, yy):
        return (zz * ny + yy, tp)

    def along(d):
        return (seq, (x + d + nx) % nx * nc + core)

    barrier = pltpu.get_barrier_semaphore()
    sibling = (seq, x * nc + (1 - core))

    def greet(target):
        pl.semaphore_signal(barrier, inc=1, device_id=target, device_id_type=MESH)

    @pl.loop(1, nz)
    def _(d):
        greet(at((z + d) % nz, y))

    greet(at((z + nz - 1) % nz, ny - 1))
    for d in range(1, ny):
        greet(at(z, (y + d) % ny))
    for d in range(1, nx):
        greet(along(d))
    greet(sibling)

    def remote(src, dst, send, recv, target):
        return pltpu.make_async_remote_copy(
            src_ref=src, dst_ref=dst, send_sem=send, recv_sem=recv, device_id=target, device_id_type=MESH
        )

    def ring_copy(way, r, h):
        step = 1 if way == 0 else -1
        origin = (z - step * (r - 1) + nz) % nz
        piece = wg.at[origin, pl.ds(h * (ny // 2), ny // 2)]
        return remote(piece, piece, w_send.at[way, r - 1, h], w_recv.at[way, r - 1, h], at((z + step + nz) % nz, y))

    last = (nz // 2, nz - 1 - nz // 2)

    def ring(r):
        for h in range(2):
            for way in range(2):
                if 2 <= r <= last[way] + 1:
                    ring_copy(way, r - 1, h).wait_recv()
                if r <= last[way]:
                    ring_copy(way, r, h).start()

    streams = (q_ref, k_ref, v_ref)
    lane16 = lax.broadcasted_iota(jnp.int32, (16, BLOCK), 1)
    row16 = lax.broadcasted_iota(jnp.int32, (16, BLOCK), 0)
    for yy in range(ny):
        edge = jnp.zeros((16, held), F32)
        for i, ref in enumerate(streams):
            part = jnp.concatenate(
                [ref[(zz * ny + yy) * OWN // 16 * 16:(zz * ny + yy) * OWN // 16 * 16 + 16, :].astype(F32)
                 [(zz * ny + yy) * OWN % 16:(zz * ny + yy) * OWN % 16 + OWN] for zz in range(nz)], axis=0).astype(BF16)
            raw[i, yy] = part
            pick = ((row16 == 2 * i) & (lane16 == BLOCK - 1)) | ((row16 == 2 * i + 1) & (lane16 == BLOCK - 2))
            edge += lax.dot_general(pick.astype(F32).astype(BF16), part, (((1,), (1,)), ((), ())),
                                    preferred_element_type=F32)
        edge_s[yy] = edge.astype(BF16)
    wide[...] = jnp.zeros_like(wide)
    for i in range(3):
        wide[3 * i:3 * i + 3, :] = taps_ref[i]
    tapst[...] = jnp.transpose(wide[...])
    taps = jnp.concatenate(
        [tapst[pl.ds(pl.multiple_of((zz * ny + y) * OWN, OWN), OWN), :] for zz in range(nz)], axis=0)
    piece = wp.shape[1]
    for yy in range(ny):
        wp[yy] = jnp.concatenate(
            [w_ref[j * OWN // 16 * 16:j * OWN // 16 * 16 + 16, :].astype(F32)[j * OWN % 16:j * OWN % 16 + OWN]
             for j in range(yy, ntp, ny)], axis=0).astype(BF16)

    pad = fwd_ref.shape[0] // 2

    def spectrum():
        columns = jnp.concatenate([rows[pl.ds(c, nb, stride=OWN), :] for c in range(OWN)], axis=1)
        left = exact(fwd_ref[...], columns)
        turned = []
        for c in range(OWN):
            re, im = left[:pad, c * BLOCK:(c + 1) * BLOCK], left[pad:, c * BLOCK:(c + 1) * BLOCK]
            turned.append(jnp.concatenate([re * turn_ref[0] - im * turn_ref[1],
                                           re * turn_ref[1] + im * turn_ref[0]], axis=1))
        return exact(jnp.concatenate(turned, axis=0), rf_ref[...])

    for b in range(nb):
        rows[b * OWN:(b + 1) * OWN, :] = h_ref[:, b * BLOCK:(b + 1) * BLOCK]
    spec[...] = spectrum()

    pl.semaphore_wait(barrier, nz - 1 + 1 - 1 + ny - 1 + nx - 1 + 1 + jnp.where(y == ny - 1, ny, 0))

    def y_copy(i, d):
        yy = (y + d) % ny
        return remote(raw.at[i, yy], got.at[i, y], y_send.at[i, d], y_recv.at[i, d], at(z, yy))

    def edge_copy(yy):
        return remote(edge_s.at[yy], edge_r, e_sem.at[1 + yy], e_sem.at[0], at((z + 1) % nz, yy))

    def wy_copy(d):
        yy = (y + d) % ny
        return remote(wp.at[yy], wg.at[z, y], wy_send.at[d], wy_recv.at[d], at(z, yy))

    own_y = [pltpu.make_async_copy(raw.at[i, y], got.at[i, y], own_sem.at[i]) for i in range(3)]
    own_w = pltpu.make_async_copy(wp.at[y], wg.at[z, y], own_sem.at[3])
    far = list(range(2, ny - 1)) + [1, ny - 1]

    @pl.when(y == ny - 1)
    def _():
        for yy in range(ny):
            edge_copy(yy).start()

    for i in (1, 2, 0):
        for d in far:
            y_copy(i, d).start()
        own_y[i].start()
    for d in far:
        wy_copy(d).start()
    own_w.start()

    lane = lax.broadcasted_iota(jnp.int32, (held, BLOCK), 1)
    edge_copy(0).wait_recv()
    wide[0:16, 0:held] = edge_r[...].astype(F32) * jnp.where(z > 0, 1.0, 0.0).astype(F32)
    before = jnp.transpose(wide[:, 0:held])

    def short(i):
        own_y[i].wait()
        for d in range(1, ny):
            y_copy(i, d).wait_recv()
        ahead1 = jnp.where(lane == 0, before[:, 2 * i:2 * i + 1], 0.0)
        ahead2 = jnp.where(lane == 0, before[:, 2 * i + 1:2 * i + 2],
                           jnp.where(lane == 1, before[:, 2 * i:2 * i + 1], 0.0))
        result = []
        for b in range(ny):
            now = got[i, b].astype(F32)
            roll1, roll2 = pltpu.roll(now, 1, 1), pltpu.roll(now, 2, 1)
            one = jnp.where(lane == 0, ahead1, roll1)
            two = jnp.where(lane < 2, ahead2, roll2)
            result.append(taps[:, 3 * i:3 * i + 1] * now + taps[:, 3 * i + 1:3 * i + 2] * one
                          + taps[:, 3 * i + 2:3 * i + 3] * two)
            ahead1, ahead2 = roll1, roll2
        return result

    pair = [a * c for a, c in zip(short(1), short(2))]
    for zz in range(nz):
        zs[zz] = jnp.concatenate([pair[b][zz * OWN:(zz + 1) * OWN] for b in range(ny)], axis=0).astype(BF16)

    def z_copy(d):
        zz = (z + d) % nz
        return remote(zs.at[zz], xin.at[z], z_send.at[d], z_recv.at[d], at(zz, y))

    own_z = pltpu.make_async_copy(zs.at[z], xin.at[z], own_sem.at[4])

    @pl.loop(1, nz)
    def _(d):
        z_copy(d).start()

    own_z.start()
    own_w.wait()
    for d in range(1, ny):
        wy_copy(d).wait_recv()
    ring(1)
    for b, value in enumerate(short(0)):
        qs[b] = value
    for r in range(2, min(3, nz // 2 + 1)):
        ring(r)
    own_z.wait()

    @pl.loop(1, nz)
    def _(d):
        z_copy(d).wait_recv()

    for zz in range(nz):
        rows[zz * ny * OWN:(zz + 1) * ny * OWN, :] = xin[zz].astype(F32)
    data = spectrum()
    for r in range(3, min(4, nz // 2 + 1)):
        ring(r)
    dr, di = data[:, :BLOCK], data[:, BLOCK:]
    fr, fi = spec[:, :BLOCK], spec[:, BLOCK:]
    mid = exact(jnp.concatenate([dr * fr - di * fi, dr * fi + di * fr], axis=1), ri_ref[...])
    turned = []
    for c in range(OWN):
        re, im = mid[c * pad:(c + 1) * pad, :BLOCK], mid[c * pad:(c + 1) * pad, BLOCK:]
        turned.append(jnp.concatenate([re * turn_ref[0] + im * turn_ref[1],
                                       im * turn_ref[0] - re * turn_ref[1]], axis=0))
    conv = exact(inv_ref[...], jnp.concatenate(turned, axis=1))
    for c in range(OWN):
        rows[pl.ds(c, nb, stride=OWN), :] = conv[:, c * BLOCK:(c + 1) * BLOCK]
    for zz in range(nz):
        ms[zz] = rows[zz * ny * OWN:(zz + 1) * ny * OWN, :].astype(BF16)

    def c_copy(d):
        zz = (z + d) % nz
        return remote(ms.at[zz], ar.at[z], c_send.at[d], c_recv.at[d], at(zz, y))

    own_c = pltpu.make_async_copy(ms.at[z], ar.at[z], own_sem.at[5])

    @pl.loop(1, nz)
    def _(d):
        c_copy(d).start()

    own_c.start()
    for r in range(4, min(6, nz // 2 + 1)):
        ring(r)
    own_c.wait()

    @pl.loop(1, nz)
    def _(d):
        c_copy(d).wait_recv()

    order = [(y + d) % ny for d in (2, 1, 3, 0)]

    def slot(d):
        return (x - d + nx) % nx * nc + core

    def x_copy(d, i):
        b = order[i]
        if d != 2:
            return remote(ga.at[tp, b], ga.at[tp, b], x_send.at[d, i], x_recv.at[d, i], along(d))
        origin, step = (slot(1), 1) if i % 2 == 0 else (slot(3), -1)
        return remote(ga.at[origin, b], ga.at[origin, b], x_send.at[d, i], x_recv.at[d, i], along(step))

    def b_copy(d, i):
        b = order[i]
        return remote(ga.at[slot(d), b], ga.at[slot(d), b], b_send.at[d, i], b_recv.at[d, i], sibling)

    depth = held
    columns = out_ref.shape[1]
    tiles, tile = total.shape[0], total.shape[2]

    def gate(i):
        b = order[i]
        mixed = jnp.concatenate(
            [rows[pl.ds(pl.multiple_of((zz * ny + b) * OWN, OWN), OWN), :] for zz in range(nz)], axis=0)
        gated = qs[b] * mixed
        if held < BLOCK:
            gated = jnp.concatenate([gated] * (BLOCK // held), axis=0)
        ga[tp, b] = jnp.transpose(gated).astype(BF16)
        for d in (1, 3):
            x_copy(d, i).start()
        b_copy(0, i).start()

    def relay(i):
        for d in (1, 3):
            x_copy(d, i).wait_recv()
        x_copy(2, i).start()
        for d in (1, 3):
            b_copy(d, i).start()

    def settle(i):
        x_copy(2, i).wait_recv()
        b_copy(2, i).start()
        for d in range(nx):
            b_copy(d, i).wait_recv()

    def partial_sum(i, n):
        lhs = jnp.concatenate([ga[p, order[i]][:, :depth] for p in range(ntp)], axis=1)
        rhs = wg[:, :, :, pl.ds(pl.multiple_of(n * tile, tile), tile)].reshape(ntp * depth, tile)
        return jnp.dot(lhs, rhs, preferred_element_type=F32)

    def half_copy(h):
        return remote(ps.at[0, pl.ds(h * (tiles // 2), tiles // 2)], half_r.at[h], r_send.at[h], r_recv.at[h],
                      at(z, (y + (1, ny - 1)[h]) % ny))

    def r_copy(h):
        return remote(ps.at[1 + h], pr.at[h], r_send.at[2 + h], r_recv.at[2 + h], at(z, (y + (1, ny - 1)[h]) % ny))

    for zz in range(nz):
        rows[zz * ny * OWN:(zz + 1) * ny * OWN, :] = ar[zz].astype(F32)

    gate(0)
    gate(1)
    for r in range(6, min(7, nz // 2 + 1)):
        ring(r)
    relay(0)
    gate(2)
    relay(1)
    gate(3)
    for r in range(7, min(8, nz // 2 + 1)):
        ring(r)
    settle(0)
    relay(2)
    for r in range(8, min(9, nz // 2 + 1)):
        ring(r)
    settle(1)
    relay(3)
    ring(nz // 2 + 1)

    @pl.loop(0, tiles)
    def _(n):
        ps[0, n] = partial_sum(0, n).astype(BF16)

    for h in range(2):
        half_copy(h).start()

    for h in range(2):
        if h == 1:
            settle(2)
        @pl.loop(0, tiles)
        def _(n):
            total[n] = partial_sum(1 + h, n)
        half_copy(h).wait_recv()
        for n in range(tiles):
            if n // (tiles // 2) == h:
                ps[1 + h, n] = (total[n] + half_r[h, n % (tiles // 2)].astype(F32)).astype(BF16)
            else:
                ps[1 + h, n] = total[n].astype(BF16)
        r_copy(h).start()

    settle(3)

    @pl.loop(0, tiles)
    def _(n):
        total[n] = partial_sum(3, n)

    for h in range(2):
        r_copy(h).wait_recv()
    for n in range(tiles):
        out_ref[:, n * tile:(n + 1) * tile] = (total[n] + pr[0, n].astype(F32) + pr[1, n].astype(F32)).astype(BF16)

    @pl.when(y == ny - 1)
    def _():
        for yy in range(ny):
            edge_copy(yy).wait_send()

    for way in range(2):
        for r in range(1, last[way] + 1):
            for h in range(2):
                ring_copy(way, r, h).wait_send()
    for d in range(1, ny):
        for i in range(3):
            y_copy(i, d).wait_send()
        wy_copy(d).wait_send()

    @pl.loop(1, nz)
    def _(d):
        z_copy(d).wait_send()
        c_copy(d).wait_send()

    for i in range(ny):
        for d in range(1, nx):
            x_copy(d, i).wait_send()
        for d in range(nx):
            b_copy(d, i).wait_send()
    for h in range(2):
        half_copy(h).wait_send()
        r_copy(h).wait_send()


def build(mesh, nz, ny, nx):
    nb, ntp = nz * ny, nx * 2
    held = OWN * nb
    group = OWN * ntp
    consts = tables(nb)

    def shards(query_proj, key_proj, value_proj, short_taps, long_filters, out_weight):
        columns = out_weight.shape[1]
        tile = min(256, columns // 2)
        pad = consts[0].shape[0] // 2
        dma = pltpu.SemaphoreType.DMA
        vmem = pltpu.VMEM
        return pl.pallas_call(
            functools.partial(kernel, nz, ny, nx),
            out_shape=jax.ShapeDtypeStruct((BLOCK, columns), BF16),
            in_specs=[pl.BlockSpec(memory_space=pltpu.VMEM)] * 11,
            out_specs=pl.BlockSpec(memory_space=pltpu.VMEM),
            scratch_shapes=[
                vmem((BLOCK, held), F32),
                vmem((held, BLOCK), F32),
                vmem((ny, 16, nz * OWN), BF16),
                vmem((16, nz * OWN), BF16),
                vmem((3, ny, nz * OWN, BLOCK), BF16),
                vmem((3, ny, nz * OWN, BLOCK), BF16),
                vmem((ny, nz * OWN, BLOCK), F32),
                vmem((nz, ny * OWN, BLOCK), BF16),
                vmem((nz, ny * OWN, BLOCK), BF16),
                vmem((held, BLOCK), F32),
                vmem((OWN * pad, 2 * BLOCK), F32),
                vmem((nz, ny * OWN, BLOCK), BF16),
                vmem((nz, ny * OWN, BLOCK), BF16),
                vmem((ntp, ny, BLOCK, BLOCK), BF16),
                vmem((ny, group // ny, columns), BF16),
                vmem((nz, ny, group // ny, columns), BF16),
                vmem((3, columns // tile, BLOCK, tile), BF16),
                vmem((2, columns // tile // 2, BLOCK, tile), BF16),
                vmem((2, columns // tile, BLOCK, tile), BF16),
                vmem((columns // tile, BLOCK, tile), F32),
                dma((1 + ny,)),
                dma((3, ny)),
                dma((3, ny)),
                dma((ny,)),
                dma((ny,)),
                dma((nz,)),
                dma((nz,)),
                dma((nz,)),
                dma((nz,)),
                dma((nx, ny)),
                dma((nx, ny)),
                dma((nx, ny)),
                dma((nx, ny)),
                dma((2, nz // 2, 2)),
                dma((2, nz // 2, 2)),
                dma((4,)),
                dma((4,)),
                dma((6,)),
            ],
            compiler_params=pltpu.CompilerParams(
                collective_id=0, has_side_effects=True, vmem_limit_bytes=60 * 1024 * 1024
            ),
        )(query_proj, key_proj, value_proj, short_taps, long_filters, out_weight, *[jnp.asarray(a) for a in consts])

    return jax.shard_map(
        shards,
        mesh=mesh,
        in_specs=(
            P("tp", "seq"),
            P("tp", "seq"),
            P("tp", "seq"),
            P(None, None, "tp"),
            P(("tp", "seq"), None),
            P("seq", "tp"),
        ),
        out_specs=P("seq", "tp"),
        check_vma=False,
    )


def solution(mesh):
    return build(mesh, mesh.shape["seq"] // 4, 4, mesh.shape["tp"] // 2)
```

```python
import functools
import math

import jax
import jax.numpy as jnp
import numpy as np
from jax import lax
from jax.experimental import pallas as pl
from jax.experimental.pallas import tpu as pltpu
from jax.sharding import PartitionSpec as P

MESH = pl.DeviceIdType.MESH
F32 = jnp.float32
BF16 = jnp.bfloat16
BLOCK = 128
OWN = 8
exact = functools.partial(jnp.dot, precision=lax.Precision.HIGHEST, preferred_element_type=F32)


def tables(blocks):
    period = 2 * blocks * BLOCK
    padded = -(-(blocks + 1) // 8) * 8
    kb = np.arange(padded)[:, None]
    live = kb <= blocks
    left = 2 * math.pi * (kb * np.arange(blocks)[None, :] % (2 * blocks)) / (2 * blocks)
    forward = np.concatenate([live * np.cos(left), -(live * np.sin(left))], axis=0)
    share = np.where((kb == 0) | (kb == blocks), 1.0, 2.0) * live / period
    inverse = np.concatenate([share * np.cos(left), -(share * np.sin(left))], axis=0).T
    twist = 2 * math.pi * (kb * np.arange(BLOCK)[None, :] % period) / period
    turn = np.stack([np.cos(twist), -np.sin(twist)])
    right = np.arange(BLOCK)
    right = 2 * math.pi * (right[:, None] * right[None, :] % BLOCK) / BLOCK
    c, s = np.cos(right), np.sin(right)
    rows = np.block([[c, -s], [s, c]])
    return [np.asarray(a, np.float32) for a in (forward, inverse, turn, rows, np.ascontiguousarray(rows.T))]


def kernel(
    nz, ny, nx,
    q_ref, k_ref, v_ref, taps_ref, h_ref, w_ref,
    fwd_ref, inv_ref, turn_ref, rf_ref, ri_ref,
    out_ref,
    wide, tapst, edge_s, edge_r, raw, got, qs, zs, xin, rows, spec, ms, ar, ga, wp, wg, ps, half_r, pr, total,
    e_sem, y_send, y_recv, wy_send, wy_recv, z_send, z_recv, c_send, c_recv, x_send, x_recv, b_send, b_recv,
    w_send, w_recv, r_send, r_recv, own_sem, ready,
):
    nc = 2
    nb = nz * ny
    ntp = nx * nc
    held = nz * OWN
    seq = lax.axis_index("seq")
    tp = lax.axis_index("tp")
    z, y = seq // ny, seq % ny
    x, core = tp // nc, tp % nc

    def at(zz, yy):
        return (zz * ny + yy, tp)

    def along(d):
        return (seq, (x + d + nx) % nx * nc + core)

    barrier = pltpu.get_barrier_semaphore()
    sibling = (seq, x * nc + (1 - core))

    def greet(target):
        pl.semaphore_signal(barrier, inc=1, device_id=target, device_id_type=MESH)

    for d in (1, nz - 1):
        greet(at((z + d) % nz, y))
    greet(at((z + nz - 1) % nz, ny - 1))
    for d in range(1, ny):
        greet(at(z, (y + d) % ny))
    for d in range(1, nx):
        greet(along(d))
    greet(sibling)

    def remote(src, dst, send, recv, target):
        return pltpu.make_async_remote_copy(
            src_ref=src, dst_ref=dst, send_sem=send, recv_sem=recv, device_id=target, device_id_type=MESH
        )

    def ring_copy(way, r, h):
        step = 1 if way == 0 else -1
        origin = (z - step * (r - 1) + nz) % nz
        piece = wg.at[origin, pl.ds(h * (ny // 2), ny // 2)]
        return remote(piece, piece, w_send.at[way, r - 1, h], w_recv.at[way, r - 1, h], at((z + step + nz) % nz, y))

    last = (nz // 2, nz - 1 - nz // 2)

    def ring(r):
        for h in range(2):
            for way in range(2):
                if 2 <= r <= last[way] + 1:
                    ring_copy(way, r - 1, h).wait_recv()
                if r <= last[way]:
                    ring_copy(way, r, h).start()

    streams = (q_ref, k_ref, v_ref)
    lane16 = lax.broadcasted_iota(jnp.int32, (16, BLOCK), 1)
    row16 = lax.broadcasted_iota(jnp.int32, (16, BLOCK), 0)
    for yy in range(ny):
        edge = jnp.zeros((16, held), F32)
        for i, ref in enumerate(streams):
            part = jnp.concatenate(
                [ref[(zz * ny + yy) * OWN // 16 * 16:(zz * ny + yy) * OWN // 16 * 16 + 16, :].astype(F32)
                 [(zz * ny + yy) * OWN % 16:(zz * ny + yy) * OWN % 16 + OWN] for zz in range(nz)], axis=0).astype(BF16)
            raw[i, yy] = part
            pick = ((row16 == 2 * i) & (lane16 == BLOCK - 1)) | ((row16 == 2 * i + 1) & (lane16 == BLOCK - 2))
            edge += lax.dot_general(pick.astype(F32).astype(BF16), part, (((1,), (1,)), ((), ())),
                                    preferred_element_type=F32)
        edge_s[yy] = edge.astype(BF16)
    wide[...] = jnp.zeros_like(wide)
    for i in range(3):
        wide[3 * i:3 * i + 3, :] = taps_ref[i]
    tapst[...] = jnp.transpose(wide[...])
    taps = jnp.concatenate(
        [tapst[pl.ds(pl.multiple_of((zz * ny + y) * OWN, OWN), OWN), :] for zz in range(nz)], axis=0)
    piece = wp.shape[1]
    for yy in range(ny):
        wp[yy] = jnp.concatenate(
            [w_ref[j * OWN // 16 * 16:j * OWN // 16 * 16 + 16, :].astype(F32)[j * OWN % 16:j * OWN % 16 + OWN]
             for j in range(yy, ntp, ny)], axis=0).astype(BF16)

    pad = fwd_ref.shape[0] // 2

    def spectrum():
        columns = jnp.concatenate([rows[pl.ds(c, nb, stride=OWN), :] for c in range(OWN)], axis=1)
        left = exact(fwd_ref[...], columns)
        turned = []
        for c in range(OWN):
            re, im = left[:pad, c * BLOCK:(c + 1) * BLOCK], left[pad:, c * BLOCK:(c + 1) * BLOCK]
            turned.append(jnp.concatenate([re * turn_ref[0] - im * turn_ref[1],
                                           re * turn_ref[1] + im * turn_ref[0]], axis=1))
        return exact(jnp.concatenate(turned, axis=0), rf_ref[...])

    for b in range(nb):
        rows[b * OWN:(b + 1) * OWN, :] = h_ref[:, b * BLOCK:(b + 1) * BLOCK]
    spec[...] = spectrum()

    pl.semaphore_wait(barrier, 2 + ny - 1 + nx - 1 + 1 + jnp.where(y == ny - 1, ny, 0))

    def word(r):
        if 2 <= r <= nz // 2:
            for way in range(2):
                if r > 2:
                    pl.semaphore_wait(ready.at[way, r - 1], 1)
                pl.semaphore_signal(ready.at[way, r], inc=1, device_id=at((z + (1, nz - 1)[way]) % nz, y),
                                    device_id_type=MESH)

    def heard():
        if nz // 2 >= 2:
            for way in range(2):
                pl.semaphore_wait(ready.at[way, nz // 2], 1)

    def y_copy(i, d):
        yy = (y + d) % ny
        return remote(raw.at[i, yy], got.at[i, y], y_send.at[i, d], y_recv.at[i, d], at(z, yy))

    def edge_copy(yy):
        return remote(edge_s.at[yy], edge_r, e_sem.at[1 + yy], e_sem.at[0], at((z + 1) % nz, yy))

    def wy_copy(d):
        yy = (y + d) % ny
        return remote(wp.at[yy], wg.at[z, y], wy_send.at[d], wy_recv.at[d], at(z, yy))

    own_y = [pltpu.make_async_copy(raw.at[i, y], got.at[i, y], own_sem.at[i]) for i in range(3)]
    own_w = pltpu.make_async_copy(wp.at[y], wg.at[z, y], own_sem.at[3])
    far = list(range(2, ny - 1)) + [1, ny - 1]

    word(2)

    @pl.when(y == ny - 1)
    def _():
        for yy in range(ny):
            edge_copy(yy).start()

    for d in far:
        wy_copy(d).start()
    for i in (1, 2, 0):
        for d in far:
            y_copy(i, d).start()
    own_w.start()
    for i in (1, 2, 0):
        own_y[i].start()
    word(3)
    own_w.wait()
    for d in range(1, ny):
        wy_copy(d).wait_recv()
    ring(1)
    word(4)

    lane = lax.broadcasted_iota(jnp.int32, (held, BLOCK), 1)
    edge_copy(0).wait_recv()
    wide[0:16, 0:held] = edge_r[...].astype(F32) * jnp.where(z > 0, 1.0, 0.0).astype(F32)
    before = jnp.transpose(wide[:, 0:held])

    def short(i):
        own_y[i].wait()
        for d in range(1, ny):
            y_copy(i, d).wait_recv()
        ahead1 = jnp.where(lane == 0, before[:, 2 * i:2 * i + 1], 0.0)
        ahead2 = jnp.where(lane == 0, before[:, 2 * i + 1:2 * i + 2],
                           jnp.where(lane == 1, before[:, 2 * i:2 * i + 1], 0.0))
        result = []
        for b in range(ny):
            now = got[i, b].astype(F32)
            roll1, roll2 = pltpu.roll(now, 1, 1), pltpu.roll(now, 2, 1)
            one = jnp.where(lane == 0, ahead1, roll1)
            two = jnp.where(lane < 2, ahead2, roll2)
            result.append(taps[:, 3 * i:3 * i + 1] * now + taps[:, 3 * i + 1:3 * i + 2] * one
                          + taps[:, 3 * i + 2:3 * i + 3] * two)
            ahead1, ahead2 = roll1, roll2
        return result

    key_short = short(1)
    word(5)
    word(6)
    value_short = short(2)
    word(7)
    word(8)
    for r in range(9, nz // 2 + 1):
        word(r)
    pair = [a * c for a, c in zip(key_short, value_short)]
    for zz in range(nz):
        zs[zz] = jnp.concatenate([pair[b][zz * OWN:(zz + 1) * OWN] for b in range(ny)], axis=0).astype(BF16)

    def z_copy(d):
        zz = (z + d) % nz
        return remote(zs.at[zz], xin.at[z], z_send.at[d], z_recv.at[d], at(zz, y))

    heard()
    own_z = pltpu.make_async_copy(zs.at[z], xin.at[z], own_sem.at[4])

    @pl.loop(1, nz)
    def _(d):
        z_copy(d).start()

    own_z.start()
    for r in range(2, min(3, nz // 2 + 1)):
        ring(r)
    for b, value in enumerate(short(0)):
        qs[b] = value
    for r in range(3, min(4, nz // 2 + 1)):
        ring(r)
    own_z.wait()

    @pl.loop(1, nz)
    def _(d):
        z_copy(d).wait_recv()

    for zz in range(nz):
        rows[zz * ny * OWN:(zz + 1) * ny * OWN, :] = xin[zz].astype(F32)
    for r in range(4, min(5, nz // 2 + 1)):
        ring(r)
    data = spectrum()
    dr, di = data[:, :BLOCK], data[:, BLOCK:]
    fr, fi = spec[:, :BLOCK], spec[:, BLOCK:]
    mid = exact(jnp.concatenate([dr * fr - di * fi, dr * fi + di * fr], axis=1), ri_ref[...])
    turned = []
    for c in range(OWN):
        re, im = mid[c * pad:(c + 1) * pad, :BLOCK], mid[c * pad:(c + 1) * pad, BLOCK:]
        turned.append(jnp.concatenate([re * turn_ref[0] + im * turn_ref[1],
                                       im * turn_ref[0] - re * turn_ref[1]], axis=0))
    conv = exact(inv_ref[...], jnp.concatenate(turned, axis=1))
    for c in range(OWN):
        rows[pl.ds(c, nb, stride=OWN), :] = conv[:, c * BLOCK:(c + 1) * BLOCK]
    for zz in range(nz):
        ms[zz] = rows[zz * ny * OWN:(zz + 1) * ny * OWN, :].astype(BF16)

    def c_copy(d):
        zz = (z + d) % nz
        return remote(ms.at[zz], ar.at[z], c_send.at[d], c_recv.at[d], at(zz, y))

    own_c = pltpu.make_async_copy(ms.at[z], ar.at[z], own_sem.at[5])

    @pl.loop(1, nz)
    def _(d):
        c_copy(d).start()

    own_c.start()
    for r in range(5, min(7, nz // 2 + 1)):
        ring(r)
    own_c.wait()

    @pl.loop(1, nz)
    def _(d):
        c_copy(d).wait_recv()

    order = [(y + d) % ny for d in (2, 1, 3, 0)]

    def slot(d):
        return (x - d + nx) % nx * nc + core

    def x_copy(d, i):
        b = order[i]
        if d != 2:
            return remote(ga.at[tp, b], ga.at[tp, b], x_send.at[d, i], x_recv.at[d, i], along(d))
        origin, step = (slot(1), 1) if i % 2 == 0 else (slot(3), -1)
        return remote(ga.at[origin, b], ga.at[origin, b], x_send.at[d, i], x_recv.at[d, i], along(step))

    def b_copy(d, i):
        b = order[i]
        return remote(ga.at[slot(d), b], ga.at[slot(d), b], b_send.at[d, i], b_recv.at[d, i], sibling)

    depth = held
    columns = out_ref.shape[1]
    tiles, tile = total.shape[0], total.shape[2]

    def gate(i):
        b = order[i]
        mixed = jnp.concatenate(
            [rows[pl.ds(pl.multiple_of((zz * ny + b) * OWN, OWN), OWN), :] for zz in range(nz)], axis=0)
        gated = qs[b] * mixed
        if held < BLOCK:
            gated = jnp.concatenate([gated] * (BLOCK // held), axis=0)
        ga[tp, b] = jnp.transpose(gated).astype(BF16)
        for d in (1, 3):
            x_copy(d, i).start()
        b_copy(0, i).start()

    def relay(i):
        for d in (1, 3):
            x_copy(d, i).wait_recv()
        x_copy(2, i).start()
        for d in (1, 3):
            b_copy(d, i).start()

    def settle(i):
        x_copy(2, i).wait_recv()
        b_copy(2, i).start()
        for d in range(nx):
            b_copy(d, i).wait_recv()

    def partial_sum(i, n):
        lhs = jnp.concatenate([ga[p, order[i]][:, :depth] for p in range(ntp)], axis=1)
        rhs = wg[:, :, :, pl.ds(pl.multiple_of(n * tile, tile), tile)].reshape(ntp * depth, tile)
        return jnp.dot(lhs, rhs, preferred_element_type=F32)

    def half_copy(h):
        return remote(ps.at[0, pl.ds(h * (tiles // 2), tiles // 2)], half_r.at[h], r_send.at[h], r_recv.at[h],
                      at(z, (y + (1, ny - 1)[h]) % ny))

    def r_copy(h, late):
        cut = pl.ds((h if late else 1 - h) * (tiles // 2), tiles // 2)
        k = 2 + 2 * h + late
        return remote(ps.at[1 + h, cut], pr.at[h, cut], r_send.at[k], r_recv.at[k],
                      at(z, (y + (1, ny - 1)[h]) % ny))

    for zz in range(nz):
        rows[zz * ny * OWN:(zz + 1) * ny * OWN, :] = ar[zz].astype(F32)

    gate(0)
    gate(1)
    relay(0)
    gate(2)
    relay(1)
    gate(3)
    for r in range(7, min(8, nz // 2 + 1)):
        ring(r)
    settle(0)
    relay(2)
    for r in range(8, min(9, nz // 2 + 1)):
        ring(r)
    settle(1)
    relay(3)
    ring(nz // 2 + 1)

    @pl.loop(0, tiles)
    def _(n):
        ps[0, n] = partial_sum(0, n).astype(BF16)

    for h in range(2):
        half_copy(h).start()

    half = tiles // 2
    for h in range(2):
        if h == 1:
            settle(2)

        @pl.loop((1 - h) * half, (1 - h) * half + half)
        def _(n):
            ps[1 + h, n] = partial_sum(1 + h, n).astype(BF16)
        r_copy(h, 0).start()

    for h in range(2):
        @pl.loop(0, half)
        def _(n):
            total[h * half + n] = partial_sum(1 + h, h * half + n)
        half_copy(h).wait_recv()
        for n in range(half):
            ps[1 + h, h * half + n] = (total[h * half + n] + half_r[h, n].astype(F32)).astype(BF16)
        r_copy(h, 1).start()

    settle(3)

    @pl.loop(0, tiles)
    def _(n):
        total[n] = partial_sum(3, n)

    for late in range(2):
        for h in range(2):
            r_copy(h, late).wait_recv()
    for n in range(tiles):
        out_ref[:, n * tile:(n + 1) * tile] = (total[n] + pr[0, n].astype(F32) + pr[1, n].astype(F32)).astype(BF16)

    @pl.when(y == ny - 1)
    def _():
        for yy in range(ny):
            edge_copy(yy).wait_send()

    for way in range(2):
        for r in range(1, last[way] + 1):
            for h in range(2):
                ring_copy(way, r, h).wait_send()
    for d in range(1, ny):
        for i in range(3):
            y_copy(i, d).wait_send()
        wy_copy(d).wait_send()

    @pl.loop(1, nz)
    def _(d):
        z_copy(d).wait_send()
        c_copy(d).wait_send()

    for i in range(ny):
        for d in range(1, nx):
            x_copy(d, i).wait_send()
        for d in range(nx):
            b_copy(d, i).wait_send()
    for h in range(2):
        half_copy(h).wait_send()
        for late in range(2):
            r_copy(h, late).wait_send()


def build(mesh, nz, ny, nx):
    nb, ntp = nz * ny, nx * 2
    held = OWN * nb
    group = OWN * ntp
    consts = tables(nb)

    def shards(query_proj, key_proj, value_proj, short_taps, long_filters, out_weight):
        columns = out_weight.shape[1]
        tile = min(256, columns // 2)
        pad = consts[0].shape[0] // 2
        dma = pltpu.SemaphoreType.DMA
        vmem = pltpu.VMEM
        return pl.pallas_call(
            functools.partial(kernel, nz, ny, nx),
            out_shape=jax.ShapeDtypeStruct((BLOCK, columns), BF16),
            in_specs=[pl.BlockSpec(memory_space=pltpu.VMEM)] * 11,
            out_specs=pl.BlockSpec(memory_space=pltpu.VMEM),
            scratch_shapes=[
                vmem((BLOCK, held), F32),
                vmem((held, BLOCK), F32),
                vmem((ny, 16, nz * OWN), BF16),
                vmem((16, nz * OWN), BF16),
                vmem((3, ny, nz * OWN, BLOCK), BF16),
                vmem((3, ny, nz * OWN, BLOCK), BF16),
                vmem((ny, nz * OWN, BLOCK), F32),
                vmem((nz, ny * OWN, BLOCK), BF16),
                vmem((nz, ny * OWN, BLOCK), BF16),
                vmem((held, BLOCK), F32),
                vmem((OWN * pad, 2 * BLOCK), F32),
                vmem((nz, ny * OWN, BLOCK), BF16),
                vmem((nz, ny * OWN, BLOCK), BF16),
                vmem((ntp, ny, BLOCK, BLOCK), BF16),
                vmem((ny, group // ny, columns), BF16),
                vmem((nz, ny, group // ny, columns), BF16),
                vmem((3, columns // tile, BLOCK, tile), BF16),
                vmem((2, columns // tile // 2, BLOCK, tile), BF16),
                vmem((2, columns // tile, BLOCK, tile), BF16),
                vmem((columns // tile, BLOCK, tile), F32),
                dma((1 + ny,)),
                dma((3, ny)),
                dma((3, ny)),
                dma((ny,)),
                dma((ny,)),
                dma((nz,)),
                dma((nz,)),
                dma((nz,)),
                dma((nz,)),
                dma((nx, ny)),
                dma((nx, ny)),
                dma((nx, ny)),
                dma((nx, ny)),
                dma((2, nz // 2, 2)),
                dma((2, nz // 2, 2)),
                dma((6,)),
                dma((6,)),
                dma((6,)),
                pltpu.SemaphoreType.REGULAR((2, nz // 2 + 1)),
            ],
            compiler_params=pltpu.CompilerParams(
                collective_id=0, has_side_effects=True, vmem_limit_bytes=60 * 1024 * 1024
            ),
        )(query_proj, key_proj, value_proj, short_taps, long_filters, out_weight, *[jnp.asarray(a) for a in consts])

    return jax.shard_map(
        shards,
        mesh=mesh,
        in_specs=(
            P("tp", "seq"),
            P("tp", "seq"),
            P("tp", "seq"),
            P(None, None, "tp"),
            P(("tp", "seq"), None),
            P("seq", "tp"),
        ),
        out_specs=P("seq", "tp"),
        check_vma=False,
    )


def solution(mesh):
    return build(mesh, mesh.shape["seq"] // 4, 4, mesh.shape["tp"] // 2)
```

```python
import functools
import math

import jax
import jax.numpy as jnp
import numpy as np
from jax import lax
from jax.experimental import pallas as pl
from jax.experimental.pallas import tpu as pltpu
from jax.sharding import PartitionSpec as P

MESH = pl.DeviceIdType.MESH
F32 = jnp.float32
BF16 = jnp.bfloat16
BLOCK = 128
OWN = 8
exact = functools.partial(jnp.dot, precision=lax.Precision.HIGHEST, preferred_element_type=F32)


def tables(blocks):
    period = 2 * blocks * BLOCK
    padded = -(-(blocks + 1) // 8) * 8
    kb = np.arange(padded)[:, None]
    live = kb <= blocks
    left = 2 * math.pi * (kb * np.arange(blocks)[None, :] % (2 * blocks)) / (2 * blocks)
    forward = np.concatenate([live * np.cos(left), -(live * np.sin(left))], axis=0)
    share = np.where((kb == 0) | (kb == blocks), 1.0, 2.0) * live / period
    inverse = np.concatenate([share * np.cos(left), -(share * np.sin(left))], axis=0).T
    twist = 2 * math.pi * (kb * np.arange(BLOCK)[None, :] % period) / period
    turn = np.stack([np.cos(twist), -np.sin(twist)])
    right = np.arange(BLOCK)
    right = 2 * math.pi * (right[:, None] * right[None, :] % BLOCK) / BLOCK
    c, s = np.cos(right), np.sin(right)
    rows = np.block([[c, -s], [s, c]])
    return [np.asarray(a, np.float32) for a in (forward, inverse, turn, rows, np.ascontiguousarray(rows.T))]


def kernel(
    nz, ny, nx,
    q_ref, k_ref, v_ref, taps_ref, h_ref, w_ref,
    fwd_ref, inv_ref, turn_ref, rf_ref, ri_ref,
    out_ref,
    wide, tapst, edge_s, edge_r, raw, got, qs, zs, xin, rows, spec, ms, ar, ga, wp, wg, ps, half_r, pr, total,
    e_sem, y_send, y_recv, wy_send, wy_recv, z_send, z_recv, c_send, c_recv, x_send, x_recv, b_send, b_recv,
    w_send, w_recv, r_send, r_recv, own_sem, ready,
):
    nc = 2
    nb = nz * ny
    ntp = nx * nc
    held = nz * OWN
    seq = lax.axis_index("seq")
    tp = lax.axis_index("tp")
    z, y = seq // ny, seq % ny
    x, core = tp // nc, tp % nc

    def at(zz, yy):
        return (zz * ny + yy, tp)

    def along(d):
        return (seq, (x + d + nx) % nx * nc + core)

    barrier = pltpu.get_barrier_semaphore()
    sibling = (seq, x * nc + (1 - core))

    def greet(target):
        pl.semaphore_signal(barrier, inc=1, device_id=target, device_id_type=MESH)

    for d in (1, nz - 1):
        greet(at((z + d) % nz, y))
    greet(at((z + nz - 1) % nz, ny - 1))
    for d in range(1, ny):
        greet(at(z, (y + d) % ny))
    for d in range(1, nx):
        greet(along(d))
    greet(sibling)

    def remote(src, dst, send, recv, target):
        return pltpu.make_async_remote_copy(
            src_ref=src, dst_ref=dst, send_sem=send, recv_sem=recv, device_id=target, device_id_type=MESH
        )

    def ring_copy(way, r, h):
        step = 1 if way == 0 else -1
        origin = (z - step * (r - 1) + nz) % nz
        piece = wg.at[origin, pl.ds(h * (ny // 2), ny // 2)]
        return remote(piece, piece, w_send.at[way, r - 1, h], w_recv.at[way, r - 1, h], at((z + step + nz) % nz, y))

    last = (nz // 2, nz - 1 - nz // 2)

    def ring(r):
        for h in range(2):
            for way in range(2):
                if 2 <= r <= last[way] + 1:
                    ring_copy(way, r - 1, h).wait_recv()
                if r <= last[way]:
                    ring_copy(way, r, h).start()

    streams = (q_ref, k_ref, v_ref)
    lane16 = lax.broadcasted_iota(jnp.int32, (16, BLOCK), 1)
    row16 = lax.broadcasted_iota(jnp.int32, (16, BLOCK), 0)
    for yy in range(ny):
        edge = jnp.zeros((16, held), F32)
        for i, ref in enumerate(streams):
            part = jnp.concatenate(
                [ref[(zz * ny + yy) * OWN // 16 * 16:(zz * ny + yy) * OWN // 16 * 16 + 16, :].astype(F32)
                 [(zz * ny + yy) * OWN % 16:(zz * ny + yy) * OWN % 16 + OWN] for zz in range(nz)], axis=0).astype(BF16)
            raw[i, yy] = part
            pick = ((row16 == 2 * i) & (lane16 == BLOCK - 1)) | ((row16 == 2 * i + 1) & (lane16 == BLOCK - 2))
            edge += lax.dot_general(pick.astype(F32).astype(BF16), part, (((1,), (1,)), ((), ())),
                                    preferred_element_type=F32)
        edge_s[yy] = edge.astype(BF16)
    wide[...] = jnp.zeros_like(wide)
    for i in range(3):
        wide[3 * i:3 * i + 3, :] = taps_ref[i]
    tapst[...] = jnp.transpose(wide[...])
    taps = jnp.concatenate(
        [tapst[pl.ds(pl.multiple_of((zz * ny + y) * OWN, OWN), OWN), :] for zz in range(nz)], axis=0)
    piece = wp.shape[1]
    for yy in range(ny):
        wp[yy] = jnp.concatenate(
            [w_ref[j * OWN // 16 * 16:j * OWN // 16 * 16 + 16, :].astype(F32)[j * OWN % 16:j * OWN % 16 + OWN]
             for j in range(yy, ntp, ny)], axis=0).astype(BF16)

    pad = fwd_ref.shape[0] // 2

    def spectrum():
        columns = jnp.concatenate([rows[pl.ds(c, nb, stride=OWN), :] for c in range(OWN)], axis=1)
        left = exact(fwd_ref[...], columns)
        turned = []
        for c in range(OWN):
            re, im = left[:pad, c * BLOCK:(c + 1) * BLOCK], left[pad:, c * BLOCK:(c + 1) * BLOCK]
            turned.append(jnp.concatenate([re * turn_ref[0] - im * turn_ref[1],
                                           re * turn_ref[1] + im * turn_ref[0]], axis=1))
        return exact(jnp.concatenate(turned, axis=0), rf_ref[...])

    for b in range(nb):
        rows[b * OWN:(b + 1) * OWN, :] = h_ref[:, b * BLOCK:(b + 1) * BLOCK]
    spec[...] = spectrum()

    pl.semaphore_wait(barrier, 2 + ny - 1 + nx - 1 + 1 + jnp.where(y == ny - 1, ny, 0))

    def word(r):
        if 2 <= r <= nz // 2:
            for way in range(2):
                if r > 2:
                    pl.semaphore_wait(ready.at[way, r - 1], 1)
                pl.semaphore_signal(ready.at[way, r], inc=1, device_id=at((z + (1, nz - 1)[way]) % nz, y),
                                    device_id_type=MESH)

    def heard():
        if nz // 2 >= 2:
            for way in range(2):
                pl.semaphore_wait(ready.at[way, nz // 2], 1)

    def y_copy(i, d):
        yy = (y + d) % ny
        return remote(raw.at[i, yy], got.at[i, y], y_send.at[i, d], y_recv.at[i, d], at(z, yy))

    def edge_copy(yy):
        return remote(edge_s.at[yy], edge_r, e_sem.at[1 + yy], e_sem.at[0], at((z + 1) % nz, yy))

    def wy_copy(d):
        yy = (y + d) % ny
        return remote(wp.at[yy], wg.at[z, y], wy_send.at[d], wy_recv.at[d], at(z, yy))

    own_y = [pltpu.make_async_copy(raw.at[i, y], got.at[i, y], own_sem.at[i]) for i in range(3)]
    own_w = pltpu.make_async_copy(wp.at[y], wg.at[z, y], own_sem.at[3])
    far = list(range(2, ny - 1)) + [1, ny - 1]

    word(2)

    @pl.when(y == ny - 1)
    def _():
        for yy in range(ny):
            edge_copy(yy).start()

    for d in far:
        wy_copy(d).start()
    for i in (1, 2, 0):
        for d in far:
            y_copy(i, d).start()
    own_w.start()
    for i in (1, 2, 0):
        own_y[i].start()
    word(3)
    own_w.wait()
    for d in range(1, ny):
        wy_copy(d).wait_recv()
    ring(1)
    word(4)

    lane = lax.broadcasted_iota(jnp.int32, (held, BLOCK), 1)
    edge_copy(0).wait_recv()
    wide[0:16, 0:held] = edge_r[...].astype(F32) * jnp.where(z > 0, 1.0, 0.0).astype(F32)
    before = jnp.transpose(wide[:, 0:held])

    def short(i):
        own_y[i].wait()
        for d in range(1, ny):
            y_copy(i, d).wait_recv()
        ahead1 = jnp.where(lane == 0, before[:, 2 * i:2 * i + 1], 0.0)
        ahead2 = jnp.where(lane == 0, before[:, 2 * i + 1:2 * i + 2],
                           jnp.where(lane == 1, before[:, 2 * i:2 * i + 1], 0.0))
        result = []
        for b in range(ny):
            now = got[i, b].astype(F32)
            roll1, roll2 = pltpu.roll(now, 1, 1), pltpu.roll(now, 2, 1)
            one = jnp.where(lane == 0, ahead1, roll1)
            two = jnp.where(lane < 2, ahead2, roll2)
            result.append(taps[:, 3 * i:3 * i + 1] * now + taps[:, 3 * i + 1:3 * i + 2] * one
                          + taps[:, 3 * i + 2:3 * i + 3] * two)
            ahead1, ahead2 = roll1, roll2
        return result

    key_short = short(1)
    for r in range(2, min(3, nz // 2 + 1)):
        ring(r)
    word(5)
    word(6)
    value_short = short(2)
    word(7)
    word(8)
    for r in range(9, nz // 2 + 1):
        word(r)
    pair = [a * c for a, c in zip(key_short, value_short)]
    for zz in range(nz):
        zs[zz] = jnp.concatenate([pair[b][zz * OWN:(zz + 1) * OWN] for b in range(ny)], axis=0).astype(BF16)

    def z_copy(d):
        zz = (z + d) % nz
        return remote(zs.at[zz], xin.at[z], z_send.at[d], z_recv.at[d], at(zz, y))

    heard()
    own_z = pltpu.make_async_copy(zs.at[z], xin.at[z], own_sem.at[4])

    @pl.loop(1, nz)
    def _(d):
        z_copy(d).start()

    own_z.start()
    for b, value in enumerate(short(0)):
        qs[b] = value
    for r in range(3, min(4, nz // 2 + 1)):
        ring(r)
    own_z.wait()

    @pl.loop(1, nz)
    def _(d):
        z_copy(d).wait_recv()

    for zz in range(nz):
        rows[zz * ny * OWN:(zz + 1) * ny * OWN, :] = xin[zz].astype(F32)
    for r in range(4, min(5, nz // 2 + 1)):
        ring(r)
    data = spectrum()
    dr, di = data[:, :BLOCK], data[:, BLOCK:]
    fr, fi = spec[:, :BLOCK], spec[:, BLOCK:]
    mid = exact(jnp.concatenate([dr * fr - di * fi, dr * fi + di * fr], axis=1), ri_ref[...])
    turned = []
    for c in range(OWN):
        re, im = mid[c * pad:(c + 1) * pad, :BLOCK], mid[c * pad:(c + 1) * pad, BLOCK:]
        turned.append(jnp.concatenate([re * turn_ref[0] + im * turn_ref[1],
                                       im * turn_ref[0] - re * turn_ref[1]], axis=0))
    conv = exact(inv_ref[...], jnp.concatenate(turned, axis=1))
    for c in range(OWN):
        rows[pl.ds(c, nb, stride=OWN), :] = conv[:, c * BLOCK:(c + 1) * BLOCK]
    for zz in range(nz):
        ms[zz] = rows[zz * ny * OWN:(zz + 1) * ny * OWN, :].astype(BF16)

    def c_copy(d):
        zz = (z + d) % nz
        return remote(ms.at[zz], ar.at[z], c_send.at[d], c_recv.at[d], at(zz, y))

    own_c = pltpu.make_async_copy(ms.at[z], ar.at[z], own_sem.at[5])

    @pl.loop(1, nz)
    def _(d):
        c_copy(d).start()

    own_c.start()
    for r in range(5, min(6, nz // 2 + 1)):
        ring(r)
    own_c.wait()

    @pl.loop(1, nz)
    def _(d):
        c_copy(d).wait_recv()

    order = [(y + d) % ny for d in (2, 1, 3, 0)]

    def slot(d):
        return (x - d + nx) % nx * nc + core

    def x_copy(d, i):
        b = order[i]
        if d != 2:
            return remote(ga.at[tp, b], ga.at[tp, b], x_send.at[d, i], x_recv.at[d, i], along(d))
        origin, step = (slot(1), 1) if i % 2 == 0 else (slot(3), -1)
        return remote(ga.at[origin, b], ga.at[origin, b], x_send.at[d, i], x_recv.at[d, i], along(step))

    def b_copy(d, i):
        b = order[i]
        return remote(ga.at[slot(d), b], ga.at[slot(d), b], b_send.at[d, i], b_recv.at[d, i], sibling)

    depth = held
    columns = out_ref.shape[1]
    tiles, tile = total.shape[0], total.shape[2]

    def gate(i):
        b = order[i]
        mixed = jnp.concatenate(
            [rows[pl.ds(pl.multiple_of((zz * ny + b) * OWN, OWN), OWN), :] for zz in range(nz)], axis=0)
        gated = qs[b] * mixed
        if held < BLOCK:
            gated = jnp.concatenate([gated] * (BLOCK // held), axis=0)
        ga[tp, b] = jnp.transpose(gated).astype(BF16)
        for d in (1, 3):
            x_copy(d, i).start()
        b_copy(0, i).start()

    def relay(i):
        for d in (1, 3):
            x_copy(d, i).wait_recv()
        x_copy(2, i).start()
        for d in (1, 3):
            b_copy(d, i).start()

    def settle(i):
        x_copy(2, i).wait_recv()
        b_copy(2, i).start()
        for d in range(nx):
            b_copy(d, i).wait_recv()

    def partial_sum(i, n):
        lhs = jnp.concatenate([ga[p, order[i]][:, :depth] for p in range(ntp)], axis=1)
        rhs = wg[:, :, :, pl.ds(pl.multiple_of(n * tile, tile), tile)].reshape(ntp * depth, tile)
        return jnp.dot(lhs, rhs, preferred_element_type=F32)

    def half_copy(h):
        return remote(ps.at[0, pl.ds(h * (tiles // 2), tiles // 2)], half_r.at[h], r_send.at[h], r_recv.at[h],
                      at(z, (y + (1, ny - 1)[h]) % ny))

    def r_copy(h, late):
        cut = pl.ds((h if late else 1 - h) * (tiles // 2), tiles // 2)
        k = 2 + 2 * h + late
        return remote(ps.at[1 + h, cut], pr.at[h, cut], r_send.at[k], r_recv.at[k],
                      at(z, (y + (1, ny - 1)[h]) % ny))

    for zz in range(nz):
        rows[zz * ny * OWN:(zz + 1) * ny * OWN, :] = ar[zz].astype(F32)
    for r in range(6, min(7, nz // 2 + 1)):
        ring(r)

    gate(0)
    gate(1)
    relay(0)
    for r in range(7, min(8, nz // 2 + 1)):
        ring(r)
    gate(2)
    relay(1)
    gate(3)
    for r in range(8, min(9, nz // 2 + 1)):
        ring(r)
    settle(0)
    relay(2)
    settle(1)
    relay(3)
    ring(nz // 2 + 1)

    @pl.loop(0, tiles)
    def _(n):
        ps[0, n] = partial_sum(0, n).astype(BF16)

    for h in range(2):
        half_copy(h).start()

    half = tiles // 2
    for h in range(2):
        if h == 1:
            settle(2)

        @pl.loop((1 - h) * half, (1 - h) * half + half)
        def _(n):
            ps[1 + h, n] = partial_sum(1 + h, n).astype(BF16)
        r_copy(h, 0).start()

    for h in range(2):
        @pl.loop(0, half)
        def _(n):
            total[h * half + n] = partial_sum(1 + h, h * half + n)
        half_copy(h).wait_recv()
        for n in range(half):
            ps[1 + h, h * half + n] = (total[h * half + n] + half_r[h, n].astype(F32)).astype(BF16)
        r_copy(h, 1).start()

    settle(3)

    @pl.loop(0, tiles)
    def _(n):
        total[n] = partial_sum(3, n)

    for late in range(2):
        for h in range(2):
            r_copy(h, late).wait_recv()
    for n in range(tiles):
        out_ref[:, n * tile:(n + 1) * tile] = (total[n] + pr[0, n].astype(F32) + pr[1, n].astype(F32)).astype(BF16)

    @pl.when(y == ny - 1)
    def _():
        for yy in range(ny):
            edge_copy(yy).wait_send()

    for way in range(2):
        for r in range(1, last[way] + 1):
            for h in range(2):
                ring_copy(way, r, h).wait_send()
    for d in range(1, ny):
        for i in range(3):
            y_copy(i, d).wait_send()
        wy_copy(d).wait_send()

    @pl.loop(1, nz)
    def _(d):
        z_copy(d).wait_send()
        c_copy(d).wait_send()

    for i in range(ny):
        for d in range(1, nx):
            x_copy(d, i).wait_send()
        for d in range(nx):
            b_copy(d, i).wait_send()
    for h in range(2):
        half_copy(h).wait_send()
        for late in range(2):
            r_copy(h, late).wait_send()


def build(mesh, nz, ny, nx):
    nb, ntp = nz * ny, nx * 2
    held = OWN * nb
    group = OWN * ntp
    consts = tables(nb)

    def shards(query_proj, key_proj, value_proj, short_taps, long_filters, out_weight):
        columns = out_weight.shape[1]
        tile = min(256, columns // 2)
        pad = consts[0].shape[0] // 2
        dma = pltpu.SemaphoreType.DMA
        vmem = pltpu.VMEM
        return pl.pallas_call(
            functools.partial(kernel, nz, ny, nx),
            out_shape=jax.ShapeDtypeStruct((BLOCK, columns), BF16),
            in_specs=[pl.BlockSpec(memory_space=pltpu.VMEM)] * 11,
            out_specs=pl.BlockSpec(memory_space=pltpu.VMEM),
            scratch_shapes=[
                vmem((BLOCK, held), F32),
                vmem((held, BLOCK), F32),
                vmem((ny, 16, nz * OWN), BF16),
                vmem((16, nz * OWN), BF16),
                vmem((3, ny, nz * OWN, BLOCK), BF16),
                vmem((3, ny, nz * OWN, BLOCK), BF16),
                vmem((ny, nz * OWN, BLOCK), F32),
                vmem((nz, ny * OWN, BLOCK), BF16),
                vmem((nz, ny * OWN, BLOCK), BF16),
                vmem((held, BLOCK), F32),
                vmem((OWN * pad, 2 * BLOCK), F32),
                vmem((nz, ny * OWN, BLOCK), BF16),
                vmem((nz, ny * OWN, BLOCK), BF16),
                vmem((ntp, ny, BLOCK, BLOCK), BF16),
                vmem((ny, group // ny, columns), BF16),
                vmem((nz, ny, group // ny, columns), BF16),
                vmem((3, columns // tile, BLOCK, tile), BF16),
                vmem((2, columns // tile // 2, BLOCK, tile), BF16),
                vmem((2, columns // tile, BLOCK, tile), BF16),
                vmem((columns // tile, BLOCK, tile), F32),
                dma((1 + ny,)),
                dma((3, ny)),
                dma((3, ny)),
                dma((ny,)),
                dma((ny,)),
                dma((nz,)),
                dma((nz,)),
                dma((nz,)),
                dma((nz,)),
                dma((nx, ny)),
                dma((nx, ny)),
                dma((nx, ny)),
                dma((nx, ny)),
                dma((2, nz // 2, 2)),
                dma((2, nz // 2, 2)),
                dma((6,)),
                dma((6,)),
                dma((6,)),
                pltpu.SemaphoreType.REGULAR((2, nz // 2 + 1)),
            ],
            compiler_params=pltpu.CompilerParams(
                collective_id=0, has_side_effects=True, vmem_limit_bytes=60 * 1024 * 1024
            ),
        )(query_proj, key_proj, value_proj, short_taps, long_filters, out_weight, *[jnp.asarray(a) for a in consts])

    return jax.shard_map(
        shards,
        mesh=mesh,
        in_specs=(
            P("tp", "seq"),
            P("tp", "seq"),
            P("tp", "seq"),
            P(None, None, "tp"),
            P(("tp", "seq"), None),
            P("seq", "tp"),
        ),
        out_specs=P("seq", "tp"),
        check_vma=False,
    )


def solution(mesh):
    return build(mesh, mesh.shape["seq"] // 4, 4, mesh.shape["tp"] // 2)
```

```python
import functools
import math

import jax
import jax.numpy as jnp
import numpy as np
from jax import lax
from jax.experimental import pallas as pl
from jax.experimental.pallas import tpu as pltpu
from jax.sharding import PartitionSpec as P

MESH = pl.DeviceIdType.MESH
F32 = jnp.float32
BF16 = jnp.bfloat16
BLOCK = 128
OWN = 8
exact = functools.partial(jnp.dot, precision=lax.Precision.HIGHEST, preferred_element_type=F32)


def tables(blocks):
    period = 2 * blocks * BLOCK
    padded = -(-(blocks + 1) // 8) * 8
    kb = np.arange(padded)[:, None]
    live = kb <= blocks
    left = 2 * math.pi * (kb * np.arange(blocks)[None, :] % (2 * blocks)) / (2 * blocks)
    forward = np.concatenate([live * np.cos(left), -(live * np.sin(left))], axis=0)
    share = np.where((kb == 0) | (kb == blocks), 1.0, 2.0) * live / period
    inverse = np.concatenate([share * np.cos(left), -(share * np.sin(left))], axis=0).T
    twist = 2 * math.pi * (kb * np.arange(BLOCK)[None, :] % period) / period
    turn = np.stack([np.cos(twist), -np.sin(twist)])
    right = np.arange(BLOCK)
    right = 2 * math.pi * (right[:, None] * right[None, :] % BLOCK) / BLOCK
    c, s = np.cos(right), np.sin(right)
    rows = np.block([[c, -s], [s, c]])
    return [np.asarray(a, np.float32) for a in (forward, inverse, turn, rows, np.ascontiguousarray(rows.T))]


def kernel(
    nz, ny, nx,
    q_ref, k_ref, v_ref, taps_ref, h_ref, w_ref,
    fwd_ref, inv_ref, turn_ref, rf_ref, ri_ref,
    out_ref,
    wide, tapst, edge_s, edge_r, raw, got, qs, zs, xin, rows, spec, ms, ar, ga, wp, wg, ps, half_r, pr, total,
    e_sem, y_send, y_recv, wy_send, wy_recv, z_send, z_recv, c_send, c_recv, x_send, x_recv, b_send, b_recv,
    w_send, w_recv, r_send, r_recv, own_sem, ready,
):
    nc = 2
    nb = nz * ny
    ntp = nx * nc
    held = nz * OWN
    seq = lax.axis_index("seq")
    tp = lax.axis_index("tp")
    z, y = seq // ny, seq % ny
    x, core = tp // nc, tp % nc

    def at(zz, yy):
        return (zz * ny + yy, tp)

    def along(d):
        return (seq, (x + d + nx) % nx * nc + core)

    barrier = pltpu.get_barrier_semaphore()
    sibling = (seq, x * nc + (1 - core))

    def greet(target):
        pl.semaphore_signal(barrier, inc=1, device_id=target, device_id_type=MESH)

    for d in (1, nz - 1):
        greet(at((z + d) % nz, y))
    greet(at((z + nz - 1) % nz, ny - 1))
    for d in range(1, ny):
        greet(at(z, (y + d) % ny))
    for d in range(1, nx):
        greet(along(d))
    greet(sibling)

    def remote(src, dst, send, recv, target):
        return pltpu.make_async_remote_copy(
            src_ref=src, dst_ref=dst, send_sem=send, recv_sem=recv, device_id=target, device_id_type=MESH
        )

    def ring_copy(way, r, h):
        step = 1 if way == 0 else -1
        origin = (z - step * (r - 1) + nz) % nz
        piece = wg.at[origin, pl.ds(h * (ny // 2), ny // 2)]
        return remote(piece, piece, w_send.at[way, r - 1, h], w_recv.at[way, r - 1, h], at((z + step + nz) % nz, y))

    last = (nz // 2, nz - 1 - nz // 2)

    def ring(r):
        for h in range(2):
            for way in range(2):
                if 2 <= r <= last[way] + 1:
                    ring_copy(way, r - 1, h).wait_recv()
                if r <= last[way]:
                    ring_copy(way, r, h).start()

    streams = (q_ref, k_ref, v_ref)
    lane16 = lax.broadcasted_iota(jnp.int32, (16, BLOCK), 1)
    row16 = lax.broadcasted_iota(jnp.int32, (16, BLOCK), 0)
    for yy in range(ny):
        edge = jnp.zeros((16, held), F32)
        for i, ref in enumerate(streams):
            part = jnp.concatenate(
                [ref[(zz * ny + yy) * OWN // 16 * 16:(zz * ny + yy) * OWN // 16 * 16 + 16, :].astype(F32)
                 [(zz * ny + yy) * OWN % 16:(zz * ny + yy) * OWN % 16 + OWN] for zz in range(nz)], axis=0).astype(BF16)
            raw[i, yy] = part
            pick = ((row16 == 2 * i) & (lane16 == BLOCK - 1)) | ((row16 == 2 * i + 1) & (lane16 == BLOCK - 2))
            edge += lax.dot_general(pick.astype(F32).astype(BF16), part, (((1,), (1,)), ((), ())),
                                    preferred_element_type=F32)
        edge_s[yy] = edge.astype(BF16)
    wide[...] = jnp.zeros_like(wide)
    for i in range(3):
        wide[3 * i:3 * i + 3, :] = taps_ref[i]
    tapst[...] = jnp.transpose(wide[...])
    taps = jnp.concatenate(
        [tapst[pl.ds(pl.multiple_of((zz * ny + y) * OWN, OWN), OWN), :] for zz in range(nz)], axis=0)
    piece = wp.shape[1]
    for yy in range(ny):
        wp[yy] = jnp.concatenate(
            [w_ref[j * OWN // 16 * 16:j * OWN // 16 * 16 + 16, :].astype(F32)[j * OWN % 16:j * OWN % 16 + OWN]
             for j in range(yy, ntp, ny)], axis=0).astype(BF16)

    pad = fwd_ref.shape[0] // 2

    def spectrum():
        columns = jnp.concatenate([rows[pl.ds(c, nb, stride=OWN), :] for c in range(OWN)], axis=1)
        left = exact(fwd_ref[...], columns)
        turned = []
        for c in range(OWN):
            re, im = left[:pad, c * BLOCK:(c + 1) * BLOCK], left[pad:, c * BLOCK:(c + 1) * BLOCK]
            turned.append(jnp.concatenate([re * turn_ref[0] - im * turn_ref[1],
                                           re * turn_ref[1] + im * turn_ref[0]], axis=1))
        return exact(jnp.concatenate(turned, axis=0), rf_ref[...])

    for b in range(nb):
        rows[b * OWN:(b + 1) * OWN, :] = h_ref[:, b * BLOCK:(b + 1) * BLOCK]
    spec[...] = spectrum()

    pl.semaphore_wait(barrier, 2 + ny - 1 + nx - 1 + 1 + jnp.where(y == ny - 1, ny, 0))

    def word(r):
        if 2 <= r <= nz // 2:
            for way in range(2):
                if r > 2:
                    pl.semaphore_wait(ready.at[way, r - 1], 1)
                pl.semaphore_signal(ready.at[way, r], inc=1, device_id=at((z + (1, nz - 1)[way]) % nz, y),
                                    device_id_type=MESH)

    def heard():
        if nz // 2 >= 2:
            for way in range(2):
                pl.semaphore_wait(ready.at[way, nz // 2], 1)

    def y_copy(i, d):
        yy = (y + d) % ny
        return remote(raw.at[i, yy], got.at[i, y], y_send.at[i, d], y_recv.at[i, d], at(z, yy))

    def edge_copy(yy):
        return remote(edge_s.at[yy], edge_r, e_sem.at[1 + yy], e_sem.at[0], at((z + 1) % nz, yy))

    def wy_copy(d):
        yy = (y + d) % ny
        return remote(wp.at[yy], wg.at[z, y], wy_send.at[d], wy_recv.at[d], at(z, yy))

    own_y = [pltpu.make_async_copy(raw.at[i, y], got.at[i, y], own_sem.at[i]) for i in range(3)]
    own_w = pltpu.make_async_copy(wp.at[y], wg.at[z, y], own_sem.at[3])
    far = list(range(2, ny - 1)) + [1, ny - 1]

    word(2)

    @pl.when(y == ny - 1)
    def _():
        for yy in range(ny):
            edge_copy(yy).start()

    for d in far:
        wy_copy(d).start()
    for i in (1, 2, 0):
        for d in far:
            y_copy(i, d).start()
    own_w.start()
    for i in (1, 2, 0):
        own_y[i].start()
    word(3)
    own_w.wait()
    for d in range(1, ny):
        wy_copy(d).wait_recv()
    ring(1)
    word(4)

    lane = lax.broadcasted_iota(jnp.int32, (held, BLOCK), 1)
    edge_copy(0).wait_recv()
    wide[0:16, 0:held] = edge_r[...].astype(F32) * jnp.where(z > 0, 1.0, 0.0).astype(F32)
    before = jnp.transpose(wide[:, 0:held])

    def short(i):
        own_y[i].wait()
        for d in range(1, ny):
            y_copy(i, d).wait_recv()
        ahead1 = jnp.where(lane == 0, before[:, 2 * i:2 * i + 1], 0.0)
        ahead2 = jnp.where(lane == 0, before[:, 2 * i + 1:2 * i + 2],
                           jnp.where(lane == 1, before[:, 2 * i:2 * i + 1], 0.0))
        result = []
        for b in range(ny):
            now = got[i, b].astype(F32)
            roll1, roll2 = pltpu.roll(now, 1, 1), pltpu.roll(now, 2, 1)
            one = jnp.where(lane == 0, ahead1, roll1)
            two = jnp.where(lane < 2, ahead2, roll2)
            result.append(taps[:, 3 * i:3 * i + 1] * now + taps[:, 3 * i + 1:3 * i + 2] * one
                          + taps[:, 3 * i + 2:3 * i + 3] * two)
            ahead1, ahead2 = roll1, roll2
        return result

    key_short = short(1)
    for r in range(2, min(3, nz // 2 + 1)):
        ring(r)
    word(5)
    word(6)
    value_short = short(2)
    word(7)
    word(8)
    for r in range(9, nz // 2 + 1):
        word(r)
    pair = [a * c for a, c in zip(key_short, value_short)]
    for zz in range(nz):
        zs[zz] = jnp.concatenate([pair[b][zz * OWN:(zz + 1) * OWN] for b in range(ny)], axis=0).astype(BF16)

    def z_copy(d):
        zz = (z + d) % nz
        return remote(zs.at[zz], xin.at[z], z_send.at[d], z_recv.at[d], at(zz, y))

    heard()
    own_z = pltpu.make_async_copy(zs.at[z], xin.at[z], own_sem.at[4])

    @pl.loop(0, nz - 1)
    def _(j):
        z_copy(nz // 2 + jnp.where(j % 2 == 0, j // 2, -(j // 2) - 1)).start()

    own_z.start()
    for b, value in enumerate(short(0)):
        qs[b] = value
    for r in range(3, min(4, nz // 2 + 1)):
        ring(r)
    own_z.wait()

    @pl.loop(1, nz)
    def _(d):
        z_copy(d).wait_recv()

    for zz in range(nz):
        rows[zz * ny * OWN:(zz + 1) * ny * OWN, :] = xin[zz].astype(F32)
    for r in range(4, min(5, nz // 2 + 1)):
        ring(r)
    data = spectrum()
    dr, di = data[:, :BLOCK], data[:, BLOCK:]
    fr, fi = spec[:, :BLOCK], spec[:, BLOCK:]
    mid = exact(jnp.concatenate([dr * fr - di * fi, dr * fi + di * fr], axis=1), ri_ref[...])
    turned = []
    for c in range(OWN):
        re, im = mid[c * pad:(c + 1) * pad, :BLOCK], mid[c * pad:(c + 1) * pad, BLOCK:]
        turned.append(jnp.concatenate([re * turn_ref[0] + im * turn_ref[1],
                                       im * turn_ref[0] - re * turn_ref[1]], axis=0))
    conv = exact(inv_ref[...], jnp.concatenate(turned, axis=1))
    for c in range(OWN):
        rows[pl.ds(c, nb, stride=OWN), :] = conv[:, c * BLOCK:(c + 1) * BLOCK]
    for zz in range(nz):
        ms[zz] = rows[zz * ny * OWN:(zz + 1) * ny * OWN, :].astype(BF16)

    def c_copy(d):
        zz = (z + d) % nz
        return remote(ms.at[zz], ar.at[z], c_send.at[d], c_recv.at[d], at(zz, y))

    own_c = pltpu.make_async_copy(ms.at[z], ar.at[z], own_sem.at[5])

    @pl.loop(0, nz - 1)
    def _(j):
        c_copy(nz // 2 + jnp.where(j % 2 == 0, j // 2, -(j // 2) - 1)).start()

    own_c.start()
    for r in range(5, min(6, nz // 2 + 1)):
        ring(r)
    own_c.wait()

    @pl.loop(1, nz)
    def _(d):
        c_copy(d).wait_recv()

    order = [(y + d) % ny for d in (2, 1, 3, 0)]

    def slot(d):
        return (x - d + nx) % nx * nc + core

    def x_copy(d, i):
        b = order[i]
        if d != 2:
            return remote(ga.at[tp, b], ga.at[tp, b], x_send.at[d, i], x_recv.at[d, i], along(d))
        origin, step = (slot(1), 1) if i % 2 == 0 else (slot(3), -1)
        return remote(ga.at[origin, b], ga.at[origin, b], x_send.at[d, i], x_recv.at[d, i], along(step))

    def b_copy(d, i):
        b = order[i]
        return remote(ga.at[slot(d), b], ga.at[slot(d), b], b_send.at[d, i], b_recv.at[d, i], sibling)

    depth = held
    columns = out_ref.shape[1]
    tiles, tile = total.shape[0], total.shape[2]

    def gate(i):
        b = order[i]
        mixed = jnp.concatenate(
            [rows[pl.ds(pl.multiple_of((zz * ny + b) * OWN, OWN), OWN), :] for zz in range(nz)], axis=0)
        gated = qs[b] * mixed
        if held < BLOCK:
            gated = jnp.concatenate([gated] * (BLOCK // held), axis=0)
        ga[tp, b] = jnp.transpose(gated).astype(BF16)
        for d in (1, 3):
            x_copy(d, i).start()
        b_copy(0, i).start()

    def relay(i):
        for d in (1, 3):
            x_copy(d, i).wait_recv()
        x_copy(2, i).start()
        for d in (1, 3):
            b_copy(d, i).start()

    def settle(i):
        x_copy(2, i).wait_recv()
        b_copy(2, i).start()
        for d in range(nx):
            b_copy(d, i).wait_recv()

    def partial_sum(i, n):
        lhs = jnp.concatenate([ga[p, order[i]][:, :depth] for p in range(ntp)], axis=1)
        rhs = wg[:, :, :, pl.ds(pl.multiple_of(n * tile, tile), tile)].reshape(ntp * depth, tile)
        return jnp.dot(lhs, rhs, preferred_element_type=F32)

    def half_copy(h):
        return remote(ps.at[0, pl.ds(h * (tiles // 2), tiles // 2)], half_r.at[h], r_send.at[h], r_recv.at[h],
                      at(z, (y + (1, ny - 1)[h]) % ny))

    def r_copy(h, late):
        cut = pl.ds((h if late else 1 - h) * (tiles // 2), tiles // 2)
        k = 2 + 2 * h + late
        return remote(ps.at[1 + h, cut], pr.at[h, cut], r_send.at[k], r_recv.at[k],
                      at(z, (y + (1, ny - 1)[h]) % ny))

    for zz in range(nz):
        rows[zz * ny * OWN:(zz + 1) * ny * OWN, :] = ar[zz].astype(F32)
    for r in range(6, min(7, nz // 2 + 1)):
        ring(r)

    gate(0)
    gate(1)
    relay(0)
    for r in range(7, min(8, nz // 2 + 1)):
        ring(r)
    gate(2)
    relay(1)
    gate(3)
    for r in range(8, min(9, nz // 2 + 1)):
        ring(r)
    settle(0)
    relay(2)
    settle(1)
    relay(3)
    ring(nz // 2 + 1)

    @pl.loop(0, tiles)
    def _(n):
        ps[0, n] = partial_sum(0, n).astype(BF16)

    for h in range(2):
        half_copy(h).start()

    half = tiles // 2
    for h in range(2):
        if h == 1:
            settle(2)

        @pl.loop((1 - h) * half, (1 - h) * half + half)
        def _(n):
            ps[1 + h, n] = partial_sum(1 + h, n).astype(BF16)
        r_copy(h, 0).start()

    for h in range(2):
        @pl.loop(0, half)
        def _(n):
            total[h * half + n] = partial_sum(1 + h, h * half + n)
        half_copy(h).wait_recv()
        for n in range(half):
            ps[1 + h, h * half + n] = (total[h * half + n] + half_r[h, n].astype(F32)).astype(BF16)
        r_copy(h, 1).start()

    settle(3)

    @pl.loop(0, tiles)
    def _(n):
        total[n] = partial_sum(3, n)

    for late in range(2):
        for h in range(2):
            r_copy(h, late).wait_recv()
    for n in range(tiles):
        out_ref[:, n * tile:(n + 1) * tile] = (total[n] + pr[0, n].astype(F32) + pr[1, n].astype(F32)).astype(BF16)

    @pl.when(y == ny - 1)
    def _():
        for yy in range(ny):
            edge_copy(yy).wait_send()

    for way in range(2):
        for r in range(1, last[way] + 1):
            for h in range(2):
                ring_copy(way, r, h).wait_send()
    for d in range(1, ny):
        for i in range(3):
            y_copy(i, d).wait_send()
        wy_copy(d).wait_send()

    @pl.loop(1, nz)
    def _(d):
        z_copy(d).wait_send()
        c_copy(d).wait_send()

    for i in range(ny):
        for d in range(1, nx):
            x_copy(d, i).wait_send()
        for d in range(nx):
            b_copy(d, i).wait_send()
    for h in range(2):
        half_copy(h).wait_send()
        for late in range(2):
            r_copy(h, late).wait_send()


def build(mesh, nz, ny, nx):
    nb, ntp = nz * ny, nx * 2
    held = OWN * nb
    group = OWN * ntp
    consts = tables(nb)

    def shards(query_proj, key_proj, value_proj, short_taps, long_filters, out_weight):
        columns = out_weight.shape[1]
        tile = min(256, columns // 2)
        pad = consts[0].shape[0] // 2
        dma = pltpu.SemaphoreType.DMA
        vmem = pltpu.VMEM
        return pl.pallas_call(
            functools.partial(kernel, nz, ny, nx),
            out_shape=jax.ShapeDtypeStruct((BLOCK, columns), BF16),
            in_specs=[pl.BlockSpec(memory_space=pltpu.VMEM)] * 11,
            out_specs=pl.BlockSpec(memory_space=pltpu.VMEM),
            scratch_shapes=[
                vmem((BLOCK, held), F32),
                vmem((held, BLOCK), F32),
                vmem((ny, 16, nz * OWN), BF16),
                vmem((16, nz * OWN), BF16),
                vmem((3, ny, nz * OWN, BLOCK), BF16),
                vmem((3, ny, nz * OWN, BLOCK), BF16),
                vmem((ny, nz * OWN, BLOCK), F32),
                vmem((nz, ny * OWN, BLOCK), BF16),
                vmem((nz, ny * OWN, BLOCK), BF16),
                vmem((held, BLOCK), F32),
                vmem((OWN * pad, 2 * BLOCK), F32),
                vmem((nz, ny * OWN, BLOCK), BF16),
                vmem((nz, ny * OWN, BLOCK), BF16),
                vmem((ntp, ny, BLOCK, BLOCK), BF16),
                vmem((ny, group // ny, columns), BF16),
                vmem((nz, ny, group // ny, columns), BF16),
                vmem((3, columns // tile, BLOCK, tile), BF16),
                vmem((2, columns // tile // 2, BLOCK, tile), BF16),
                vmem((2, columns // tile, BLOCK, tile), BF16),
                vmem((columns // tile, BLOCK, tile), F32),
                dma((1 + ny,)),
                dma((3, ny)),
                dma((3, ny)),
                dma((ny,)),
                dma((ny,)),
                dma((nz,)),
                dma((nz,)),
                dma((nz,)),
                dma((nz,)),
                dma((nx, ny)),
                dma((nx, ny)),
                dma((nx, ny)),
                dma((nx, ny)),
                dma((2, nz // 2, 2)),
                dma((2, nz // 2, 2)),
                dma((6,)),
                dma((6,)),
                dma((6,)),
                pltpu.SemaphoreType.REGULAR((2, nz // 2 + 1)),
            ],
            compiler_params=pltpu.CompilerParams(
                collective_id=0, has_side_effects=True, vmem_limit_bytes=60 * 1024 * 1024
            ),
        )(query_proj, key_proj, value_proj, short_taps, long_filters, out_weight, *[jnp.asarray(a) for a in consts])

    return jax.shard_map(
        shards,
        mesh=mesh,
        in_specs=(
            P("tp", "seq"),
            P("tp", "seq"),
            P("tp", "seq"),
            P(None, None, "tp"),
            P(("tp", "seq"), None),
            P("seq", "tp"),
        ),
        out_specs=P("seq", "tp"),
        check_vma=False,
    )


def solution(mesh):
    return build(mesh, mesh.shape["seq"] // 4, 4, mesh.shape["tp"] // 2)
```

```python
import functools
import math

import jax
import jax.numpy as jnp
import numpy as np
from jax import lax
from jax.experimental import pallas as pl
from jax.experimental.pallas import tpu as pltpu
from jax.sharding import PartitionSpec as P

MESH = pl.DeviceIdType.MESH
F32 = jnp.float32
BF16 = jnp.bfloat16
BLOCK = 128
OWN = 8
exact = functools.partial(jnp.dot, precision=lax.Precision.HIGHEST, preferred_element_type=F32)


def tables(blocks):
    period = 2 * blocks * BLOCK
    padded = -(-(blocks + 1) // 8) * 8
    kb = np.arange(padded)[:, None]
    live = kb <= blocks
    left = 2 * math.pi * (kb * np.arange(blocks)[None, :] % (2 * blocks)) / (2 * blocks)
    forward = np.concatenate([live * np.cos(left), -(live * np.sin(left))], axis=0)
    share = np.where((kb == 0) | (kb == blocks), 1.0, 2.0) * live / period
    inverse = np.concatenate([share * np.cos(left), -(share * np.sin(left))], axis=0).T
    twist = 2 * math.pi * (kb * np.arange(BLOCK)[None, :] % period) / period
    turn = np.stack([np.cos(twist), -np.sin(twist)])
    right = np.arange(BLOCK)
    right = 2 * math.pi * (right[:, None] * right[None, :] % BLOCK) / BLOCK
    c, s = np.cos(right), np.sin(right)
    rows = np.block([[c, -s], [s, c]])
    return [np.asarray(a, np.float32) for a in (forward, inverse, turn, rows, np.ascontiguousarray(rows.T))]


def kernel(
    nz, ny, nx,
    q_ref, k_ref, v_ref, taps_ref, h_ref, w_ref,
    fwd_ref, inv_ref, turn_ref, rf_ref, ri_ref,
    out_ref,
    wide, tapst, edge_s, edge_r, raw, got, qs, zs, xin, rows, spec, ms, ar, ga, wp, wg, ps, half_r, pr, total,
    e_sem, y_send, y_recv, wy_send, wy_recv, z_send, z_recv, c_send, c_recv, x_send, x_recv, b_send, b_recv,
    w_send, w_recv, r_send, r_recv, own_sem, ready,
):
    nc = 2
    nb = nz * ny
    ntp = nx * nc
    held = nz * OWN
    seq = lax.axis_index("seq")
    tp = lax.axis_index("tp")
    z, y = seq // ny, seq % ny
    x, core = tp // nc, tp % nc

    def at(zz, yy):
        return (zz * ny + yy, tp)

    def along(d):
        return (seq, (x + d + nx) % nx * nc + core)

    barrier = pltpu.get_barrier_semaphore()
    sibling = (seq, x * nc + (1 - core))

    def greet(target):
        pl.semaphore_signal(barrier, inc=1, device_id=target, device_id_type=MESH)

    for d in (1, nz - 1):
        greet(at((z + d) % nz, y))
    greet(at((z + nz - 1) % nz, ny - 1))
    for d in range(1, ny):
        greet(at(z, (y + d) % ny))
    for d in range(1, nx):
        greet(along(d))
    greet(sibling)

    def remote(src, dst, send, recv, target):
        return pltpu.make_async_remote_copy(
            src_ref=src, dst_ref=dst, send_sem=send, recv_sem=recv, device_id=target, device_id_type=MESH
        )

    def ring_copy(way, r, h):
        step = 1 if way == 0 else -1
        origin = (z - step * (r - 1) + nz) % nz
        piece = wg.at[origin, pl.ds(h * (ny // 2), ny // 2)]
        return remote(piece, piece, w_send.at[way, r - 1, h], w_recv.at[way, r - 1, h], at((z + step + nz) % nz, y))

    last = (nz // 2, nz - 1 - nz // 2)

    def ring(r):
        for h in range(2):
            for way in range(2):
                if 2 <= r <= last[way] + 1:
                    ring_copy(way, r - 1, h).wait_recv()
                if r <= last[way]:
                    ring_copy(way, r, h).start()

    streams = (q_ref, k_ref, v_ref)
    lane16 = lax.broadcasted_iota(jnp.int32, (16, BLOCK), 1)
    row16 = lax.broadcasted_iota(jnp.int32, (16, BLOCK), 0)
    for yy in range(ny):
        edge = jnp.zeros((16, held), F32)
        for i, ref in enumerate(streams):
            part = jnp.concatenate(
                [ref[(zz * ny + yy) * OWN // 16 * 16:(zz * ny + yy) * OWN // 16 * 16 + 16, :].astype(F32)
                 [(zz * ny + yy) * OWN % 16:(zz * ny + yy) * OWN % 16 + OWN] for zz in range(nz)], axis=0).astype(BF16)
            raw[i, yy] = part
            pick = ((row16 == 2 * i) & (lane16 == BLOCK - 1)) | ((row16 == 2 * i + 1) & (lane16 == BLOCK - 2))
            edge += lax.dot_general(pick.astype(F32).astype(BF16), part, (((1,), (1,)), ((), ())),
                                    preferred_element_type=F32)
        edge_s[yy] = edge.astype(BF16)
    wide[...] = jnp.zeros_like(wide)
    for i in range(3):
        wide[3 * i:3 * i + 3, :] = taps_ref[i]
    tapst[...] = jnp.transpose(wide[...])
    taps = jnp.concatenate(
        [tapst[pl.ds(pl.multiple_of((zz * ny + y) * OWN, OWN), OWN), :] for zz in range(nz)], axis=0)
    piece = wp.shape[1]
    for yy in range(ny):
        wp[yy] = jnp.concatenate(
            [w_ref[j * OWN // 16 * 16:j * OWN // 16 * 16 + 16, :].astype(F32)[j * OWN % 16:j * OWN % 16 + OWN]
             for j in range(yy, ntp, ny)], axis=0).astype(BF16)

    pad = fwd_ref.shape[0] // 2

    def spectrum():
        columns = jnp.concatenate([rows[pl.ds(c, nb, stride=OWN), :] for c in range(OWN)], axis=1)
        left = exact(fwd_ref[...], columns)
        turned = []
        for c in range(OWN):
            re, im = left[:pad, c * BLOCK:(c + 1) * BLOCK], left[pad:, c * BLOCK:(c + 1) * BLOCK]
            turned.append(jnp.concatenate([re * turn_ref[0] - im * turn_ref[1],
                                           re * turn_ref[1] + im * turn_ref[0]], axis=1))
        return exact(jnp.concatenate(turned, axis=0), rf_ref[...])

    for b in range(nb):
        rows[b * OWN:(b + 1) * OWN, :] = h_ref[:, b * BLOCK:(b + 1) * BLOCK]
    spec[...] = spectrum()

    pl.semaphore_wait(barrier, 2 + ny - 1 + nx - 1 + 1 + jnp.where(y == ny - 1, ny, 0))

    def word(r):
        if 2 <= r <= nz // 2:
            for way in range(2):
                if r > 2:
                    pl.semaphore_wait(ready.at[way, r - 1], 1)
                pl.semaphore_signal(ready.at[way, r], inc=1, device_id=at((z + (1, nz - 1)[way]) % nz, y),
                                    device_id_type=MESH)

    def heard():
        if nz // 2 >= 2:
            for way in range(2):
                pl.semaphore_wait(ready.at[way, nz // 2], 1)

    def y_copy(i, d):
        yy = (y + d) % ny
        return remote(raw.at[i, yy], got.at[i, y], y_send.at[i, d], y_recv.at[i, d], at(z, yy))

    def edge_copy(yy):
        return remote(edge_s.at[yy], edge_r, e_sem.at[1 + yy], e_sem.at[0], at((z + 1) % nz, yy))

    def wy_copy(d):
        yy = (y + d) % ny
        return remote(wp.at[yy], wg.at[z, y], wy_send.at[d], wy_recv.at[d], at(z, yy))

    own_y = [pltpu.make_async_copy(raw.at[i, y], got.at[i, y], own_sem.at[i]) for i in range(3)]
    own_w = pltpu.make_async_copy(wp.at[y], wg.at[z, y], own_sem.at[3])
    far = list(range(2, ny - 1)) + [1, ny - 1]

    word(2)

    @pl.when(y == ny - 1)
    def _():
        for yy in range(ny):
            edge_copy(yy).start()

    for d in far:
        wy_copy(d).start()
    for i in (1, 2, 0):
        for d in far:
            y_copy(i, d).start()
    own_w.start()
    for i in (1, 2, 0):
        own_y[i].start()
    word(3)
    own_w.wait()
    for d in range(1, ny):
        wy_copy(d).wait_recv()
    ring(1)
    word(4)

    lane = lax.broadcasted_iota(jnp.int32, (held, BLOCK), 1)
    edge_copy(0).wait_recv()
    wide[0:16, 0:held] = edge_r[...].astype(F32) * jnp.where(z > 0, 1.0, 0.0).astype(F32)
    before = jnp.transpose(wide[:, 0:held])

    def short(i):
        own_y[i].wait()
        for d in range(1, ny):
            y_copy(i, d).wait_recv()
        ahead1 = jnp.where(lane == 0, before[:, 2 * i:2 * i + 1], 0.0)
        ahead2 = jnp.where(lane == 0, before[:, 2 * i + 1:2 * i + 2],
                           jnp.where(lane == 1, before[:, 2 * i:2 * i + 1], 0.0))
        result = []
        for b in range(ny):
            now = got[i, b].astype(F32)
            roll1, roll2 = pltpu.roll(now, 1, 1), pltpu.roll(now, 2, 1)
            one = jnp.where(lane == 0, ahead1, roll1)
            two = jnp.where(lane < 2, ahead2, roll2)
            result.append(taps[:, 3 * i:3 * i + 1] * now + taps[:, 3 * i + 1:3 * i + 2] * one
                          + taps[:, 3 * i + 2:3 * i + 3] * two)
            ahead1, ahead2 = roll1, roll2
        return result

    key_short = short(1)
    for r in range(2, min(3, nz // 2 + 1)):
        ring(r)
    word(5)
    word(6)
    value_short = short(2)
    word(7)
    word(8)
    for r in range(9, nz // 2 + 1):
        word(r)
    pair = [a * c for a, c in zip(key_short, value_short)]
    for zz in range(nz):
        zs[zz] = jnp.concatenate([pair[b][zz * OWN:(zz + 1) * OWN] for b in range(ny)], axis=0).astype(BF16)

    def z_copy(d):
        zz = (z + d) % nz
        return remote(zs.at[zz], xin.at[z], z_send.at[d], z_recv.at[d], at(zz, y))

    heard()
    own_z = pltpu.make_async_copy(zs.at[z], xin.at[z], own_sem.at[4])

    @pl.loop(0, nz - 1)
    def _(j):
        z_copy(nz // 2 + jnp.where(j % 2 == 0, j // 2, -(j // 2) - 1)).start()

    own_z.start()
    for b, value in enumerate(short(0)):
        qs[b] = value
    for r in range(3, min(4, nz // 2 + 1)):
        ring(r)
    own_z.wait()

    @pl.loop(1, nz)
    def _(d):
        z_copy(d).wait_recv()

    for zz in range(nz):
        rows[zz * ny * OWN:(zz + 1) * ny * OWN, :] = xin[zz].astype(F32)
    for r in range(4, min(5, nz // 2 + 1)):
        ring(r)
    data = spectrum()
    dr, di = data[:, :BLOCK], data[:, BLOCK:]
    fr, fi = spec[:, :BLOCK], spec[:, BLOCK:]
    mid = exact(jnp.concatenate([dr * fr - di * fi, dr * fi + di * fr], axis=1), ri_ref[...])
    turned = []
    for c in range(OWN):
        re, im = mid[c * pad:(c + 1) * pad, :BLOCK], mid[c * pad:(c + 1) * pad, BLOCK:]
        turned.append(jnp.concatenate([re * turn_ref[0] + im * turn_ref[1],
                                       im * turn_ref[0] - re * turn_ref[1]], axis=0))
    conv = exact(inv_ref[...], jnp.concatenate(turned, axis=1))
    for c in range(OWN):
        rows[pl.ds(c, nb, stride=OWN), :] = conv[:, c * BLOCK:(c + 1) * BLOCK]
    for zz in range(nz):
        ms[zz] = rows[zz * ny * OWN:(zz + 1) * ny * OWN, :].astype(BF16)

    def c_copy(d):
        zz = (z + d) % nz
        return remote(ms.at[zz], ar.at[z], c_send.at[d], c_recv.at[d], at(zz, y))

    own_c = pltpu.make_async_copy(ms.at[z], ar.at[z], own_sem.at[5])

    @pl.loop(0, nz - 1)
    def _(j):
        c_copy(nz // 2 + jnp.where(j % 2 == 0, j // 2, -(j // 2) - 1)).start()

    own_c.start()
    for r in range(5, min(6, nz // 2 + 1)):
        ring(r)
    own_c.wait()

    @pl.loop(1, nz)
    def _(d):
        c_copy(d).wait_recv()

    order = [(y + d) % ny for d in (2, 1, 3, 0)]

    def slot(d):
        return (x - d + nx) % nx * nc + core

    def x_copy(d, i):
        b = order[i]
        if d != 2:
            return remote(ga.at[tp, b], ga.at[tp, b], x_send.at[d, i], x_recv.at[d, i], along(d))
        origin, step = (slot(1), 1) if i % 2 == 0 else (slot(3), -1)
        return remote(ga.at[origin, b], ga.at[origin, b], x_send.at[d, i], x_recv.at[d, i], along(step))

    def b_copy(d, i):
        b = order[i]
        return remote(ga.at[slot(d), b], ga.at[slot(d), b], b_send.at[d, i], b_recv.at[d, i], sibling)

    depth = held
    columns = out_ref.shape[1]
    tiles, tile = total.shape[0], total.shape[2]

    def gate(i):
        b = order[i]
        mixed = jnp.concatenate(
            [rows[pl.ds(pl.multiple_of((zz * ny + b) * OWN, OWN), OWN), :] for zz in range(nz)], axis=0)
        gated = qs[b] * mixed
        if held < BLOCK:
            gated = jnp.concatenate([gated] * (BLOCK // held), axis=0)
        ga[tp, b] = jnp.transpose(gated).astype(BF16)
        for d in (1, 3):
            x_copy(d, i).start()
        b_copy(0, i).start()

    def relay(i):
        for d in (1, 3):
            x_copy(d, i).wait_recv()
        x_copy(2, i).start()
        for d in (1, 3):
            b_copy(d, i).start()

    def settle(i):
        x_copy(2, i).wait_recv()
        b_copy(2, i).start()
        for d in range(nx):
            b_copy(d, i).wait_recv()

    def partial_sum(i, n):
        lhs = jnp.concatenate([ga[p, order[i]][:, :depth] for p in range(ntp)], axis=1)
        rhs = wg[:, :, :, pl.ds(pl.multiple_of(n * tile, tile), tile)].reshape(ntp * depth, tile)
        return jnp.dot(lhs, rhs, preferred_element_type=F32)

    def half_copy(h):
        return remote(ps.at[0, pl.ds(h * (tiles // 2), tiles // 2)], half_r.at[h], r_send.at[h], r_recv.at[h],
                      at(z, (y + (1, ny - 1)[h]) % ny))

    def r_copy(h, late):
        cut = pl.ds((h if late else 1 - h) * (tiles // 2), tiles // 2)
        k = 2 + 2 * h + late
        return remote(ps.at[1 + h, cut], pr.at[h, cut], r_send.at[k], r_recv.at[k],
                      at(z, (y + (1, ny - 1)[h]) % ny))

    for zz in range(nz):
        rows[zz * ny * OWN:(zz + 1) * ny * OWN, :] = ar[zz].astype(F32)
    for r in range(6, min(7, nz // 2 + 1)):
        ring(r)

    gate(0)
    gate(1)
    for r in range(7, min(8, nz // 2 + 1)):
        ring(r)
    relay(0)
    gate(2)
    relay(1)
    for r in range(8, min(9, nz // 2 + 1)):
        ring(r)
    gate(3)
    settle(0)
    relay(2)
    settle(1)
    relay(3)
    ring(nz // 2 + 1)

    @pl.loop(0, tiles)
    def _(n):
        ps[0, n] = partial_sum(0, n).astype(BF16)

    for h in range(2):
        half_copy(h).start()

    half = tiles // 2
    for h in range(2):
        if h == 1:
            settle(2)

        @pl.loop((1 - h) * half, (1 - h) * half + half)
        def _(n):
            ps[1 + h, n] = partial_sum(1 + h, n).astype(BF16)
        r_copy(h, 0).start()

    for h in range(2):
        @pl.loop(0, half)
        def _(n):
            total[h * half + n] = partial_sum(1 + h, h * half + n)
        half_copy(h).wait_recv()
        for n in range(half):
            ps[1 + h, h * half + n] = (total[h * half + n] + half_r[h, n].astype(F32)).astype(BF16)
        r_copy(h, 1).start()

    settle(3)

    @pl.loop(0, tiles)
    def _(n):
        total[n] = partial_sum(3, n)

    for late in range(2):
        for h in range(2):
            r_copy(h, late).wait_recv()
    for n in range(tiles):
        out_ref[:, n * tile:(n + 1) * tile] = (total[n] + pr[0, n].astype(F32) + pr[1, n].astype(F32)).astype(BF16)

    @pl.when(y == ny - 1)
    def _():
        for yy in range(ny):
            edge_copy(yy).wait_send()

    for way in range(2):
        for r in range(1, last[way] + 1):
            for h in range(2):
                ring_copy(way, r, h).wait_send()
    for d in range(1, ny):
        for i in range(3):
            y_copy(i, d).wait_send()
        wy_copy(d).wait_send()

    @pl.loop(1, nz)
    def _(d):
        z_copy(d).wait_send()
        c_copy(d).wait_send()

    for i in range(ny):
        for d in range(1, nx):
            x_copy(d, i).wait_send()
        for d in range(nx):
            b_copy(d, i).wait_send()
    for h in range(2):
        half_copy(h).wait_send()
        for late in range(2):
            r_copy(h, late).wait_send()


def build(mesh, nz, ny, nx):
    nb, ntp = nz * ny, nx * 2
    held = OWN * nb
    group = OWN * ntp
    consts = tables(nb)

    def shards(query_proj, key_proj, value_proj, short_taps, long_filters, out_weight):
        columns = out_weight.shape[1]
        tile = min(256, columns // 2)
        pad = consts[0].shape[0] // 2
        dma = pltpu.SemaphoreType.DMA
        vmem = pltpu.VMEM
        return pl.pallas_call(
            functools.partial(kernel, nz, ny, nx),
            out_shape=jax.ShapeDtypeStruct((BLOCK, columns), BF16),
            in_specs=[pl.BlockSpec(memory_space=pltpu.VMEM)] * 11,
            out_specs=pl.BlockSpec(memory_space=pltpu.VMEM),
            scratch_shapes=[
                vmem((BLOCK, held), F32),
                vmem((held, BLOCK), F32),
                vmem((ny, 16, nz * OWN), BF16),
                vmem((16, nz * OWN), BF16),
                vmem((3, ny, nz * OWN, BLOCK), BF16),
                vmem((3, ny, nz * OWN, BLOCK), BF16),
                vmem((ny, nz * OWN, BLOCK), F32),
                vmem((nz, ny * OWN, BLOCK), BF16),
                vmem((nz, ny * OWN, BLOCK), BF16),
                vmem((held, BLOCK), F32),
                vmem((OWN * pad, 2 * BLOCK), F32),
                vmem((nz, ny * OWN, BLOCK), BF16),
                vmem((nz, ny * OWN, BLOCK), BF16),
                vmem((ntp, ny, BLOCK, BLOCK), BF16),
                vmem((ny, group // ny, columns), BF16),
                vmem((nz, ny, group // ny, columns), BF16),
                vmem((3, columns // tile, BLOCK, tile), BF16),
                vmem((2, columns // tile // 2, BLOCK, tile), BF16),
                vmem((2, columns // tile, BLOCK, tile), BF16),
                vmem((columns // tile, BLOCK, tile), F32),
                dma((1 + ny,)),
                dma((3, ny)),
                dma((3, ny)),
                dma((ny,)),
                dma((ny,)),
                dma((nz,)),
                dma((nz,)),
                dma((nz,)),
                dma((nz,)),
                dma((nx, ny)),
                dma((nx, ny)),
                dma((nx, ny)),
                dma((nx, ny)),
                dma((2, nz // 2, 2)),
                dma((2, nz // 2, 2)),
                dma((6,)),
                dma((6,)),
                dma((6,)),
                pltpu.SemaphoreType.REGULAR((2, nz // 2 + 1)),
            ],
            compiler_params=pltpu.CompilerParams(
                collective_id=0, has_side_effects=True, vmem_limit_bytes=60 * 1024 * 1024
            ),
        )(query_proj, key_proj, value_proj, short_taps, long_filters, out_weight, *[jnp.asarray(a) for a in consts])

    return jax.shard_map(
        shards,
        mesh=mesh,
        in_specs=(
            P("tp", "seq"),
            P("tp", "seq"),
            P("tp", "seq"),
            P(None, None, "tp"),
            P(("tp", "seq"), None),
            P("seq", "tp"),
        ),
        out_specs=P("seq", "tp"),
        check_vma=False,
    )


def solution(mesh):
    return build(mesh, mesh.shape["seq"] // 4, 4, mesh.shape["tp"] // 2)
```
